32 devices in a mesh: shot: 8 (over z, x), gx: 2 (over y), gy: 2 (over core).
Axes of the slice: x: 2, y: 2, z: 4, core: 2. Of those that a mesh axis runs over, the one named last changes fastest.
Arguments:
- state: float32 [8, 4, 32, 6144], P('shot', None, 'gx', 'gy'), may hold values from -4 to 4
- velocity: float32 [32, 96, 64], P('gx', 'gy', 'shot'), may hold values from 0.03 to 0.18
- image_prior: float32 [32, 96, 64], P('gx', 'gy', 'shot'), may hold values from -6 to 6
- source_x: int32 [8], P('shot'), may hold values from 0 to 31
- source_y: int32 [8], P('shot'), may hold values from 0 to 95
- wavelet: float32 [8, 2], P('shot'), may hold values from -16 to 16
- receiver_x: int32 [8, 4096], P('shot'), may hold values from 0 to 31
- receiver_y: int32 [8, 4096], P('shot'), may hold values from 0 to 95
- recorded: float32 [8, 2, 4096], P('shot'), may hold values from -12 to 12
Outputs:
- state_out: float32 [8, 4, 32, 6144], P('shot', None, 'gx', 'gy')
- image: float32 [32, 96, 64], P('gx', 'gy', 'shot')
The draws below stay inside these ranges and needn't reach their ends.
All inputs are finite; a program needn't handle non-finite values.
Results may differ from the reference program's by a relative error of at most 0.00012.
Values sent between devices are 32-bit elements; how exact they have to be, the bound alone decides.
A program may use at most 64 MiB of HBM per device.

```python
import math
import jax
import jax.numpy as jnp
from jax import lax

NREC = 4096
STEPS = 2
SRC_Z = 4
REC_Z = 2
GROUPS = 8
NX = 32
NY = 96
NZ = 64


def place_ends(values, own_key, low, largest):
    index_at = [jax.random.randint(jax.random.fold_in(own_key, axis), (), 0, length) for axis, length in enumerate(values.shape)]
    main_axis = values.shape.index(max(values.shape))
    next_to = index_at[:main_axis] + [(index_at[main_axis] + 1) % values.shape[main_axis]] + index_at[main_axis + 1:]
    return values.at[tuple(index_at)].set(low).at[tuple(next_to)].set(largest)


def level_of(own_key, dims, split, least, top_value):
    loudness = 1.0
    for dim, shards_of in split:
        draws = jax.random.uniform(jax.random.fold_in(jax.random.fold_in(own_key, 6), dim), (shards_of,), jnp.float32, least / len(split), top_value / len(split))
        loudness = loudness * jnp.repeat(jnp.exp(draws), dims[dim] // shards_of).reshape((-1,) + (1,) * (len(dims) - 1 - dim))
    return loudness


def normal_values(stream_key, dims, spread, limit, pieces=(), kind=jnp.bfloat16):
    drawn = jax.random.normal(stream_key, dims, jnp.float32) * spread
    if len(pieces) > 0:
        drawn = level_of(stream_key, dims, pieces, -0.22, 0.18) * drawn
    return jnp.clip(drawn, min=-limit, max=limit).astype(kind)


def setup_inputs(seed: int = 0) -> dict:
    seeds = jax.random.split(jax.random.key(seed), 10)
    state = normal_values(seeds[0], (GROUPS, 4, NX, NY * NZ), 0.5, 4.0, ((0, 8), (2, 2), (3, 2)), jnp.float32)
    velocity = jnp.clip(jnp.exp(math.log(0.18) - 1.7917595 * jax.random.uniform(seeds[1], (NX, NY, NZ), jnp.float32) ** level_of(seeds[1], (NX, NY, NZ), ((0, 2), (1, 2), (2, 8)), -0.2, 0.2)), 0.03, 0.18)
    image_prior = normal_values(seeds[2], (NX, NY, NZ), 1.0, 6.0, ((0, 2), (1, 2), (2, 8)), jnp.float32)
    source_x = place_ends(jax.random.randint(seeds[3], (GROUPS,), 0, NX), jax.random.fold_in(seeds[3], 1), 0, NX - 1).astype(jnp.int32)
    source_y = place_ends(jax.random.randint(seeds[4], (GROUPS,), 0, NY), jax.random.fold_in(seeds[4], 1), 0, NY - 1).astype(jnp.int32)
    wavelet = normal_values(seeds[5], (GROUPS, STEPS), 4.0, 16.0, ((0, 8),), jnp.float32)
    receiver_x = place_ends(jax.random.randint(seeds[6], (GROUPS, NREC), 0, NX), jax.random.fold_in(seeds[6], 1), 0, NX - 1).astype(jnp.int32)
    receiver_y = place_ends(jax.random.randint(seeds[7], (GROUPS, NREC), 0, NY), jax.random.fold_in(seeds[7], 1), 0, NY - 1).astype(jnp.int32)
    recorded = normal_values(seeds[8], (GROUPS, STEPS, NREC), 2.0, 12.0, ((0, 8),), jnp.float32)
    return dict(state=state, velocity=velocity, image_prior=image_prior, source_x=source_x, source_y=source_y, wavelet=wavelet, receiver_x=receiver_x, receiver_y=receiver_y, recorded=recorded)


STENCIL = (-205.0 / 72.0, 8.0 / 5.0, -1.0 / 5.0, 8.0 / 315.0, -1.0 / 560.0)


def laplace(extended):
    width_x = extended.shape[1] - 8
    width_y = extended.shape[2] - 8
    depth = extended.shape[3]
    padded = jnp.pad(extended, ((0, 0), (0, 0), (0, 0), (4, 4)))

    def shifted(dx, dy, dz):
        return padded[:, 4 + dx:4 + dx + width_x, 4 + dy:4 + dy + width_y, 4 + dz:4 + dz + depth]

    summed = (3.0 * STENCIL[0]) * shifted(0, 0, 0)
    for offset in range(1, 5):
        summed = summed + STENCIL[offset] * (shifted(offset, 0, 0) + shifted(-offset, 0, 0) + shifted(0, offset, 0) + shifted(0, -offset, 0) + shifted(0, 0, offset) + shifted(0, 0, -offset))
    return summed


def reference(state, velocity, image_prior, source_x, source_y, wavelet, receiver_x, receiver_y, recorded):
    def one_group(inputs):
        merged, sx, sy, wave, rx, ry, data = inputs
        fields = merged.reshape((4, NX, NY, NZ))
        previous = jnp.stack((fields[0], fields[2]))
        current = jnp.stack((fields[1], fields[3]))
        image_sum = jnp.zeros((NX, NY, NZ), jnp.float32)
        for step_index in range(STEPS):
            extended = jnp.pad(current, ((0, 0), (4, 4), (4, 4), (0, 0)))
            advanced = 2.0 * current - previous + velocity[None] * laplace(extended)
            src_plane = jnp.zeros((NX, NY), jnp.float32).at[sx, sy].add(wave[step_index])
            rec_plane = jnp.zeros((NX, NY), jnp.float32).at[rx, ry].add(data[step_index])
            advanced = advanced.at[0, :, :, SRC_Z].add(src_plane)
            advanced = advanced.at[1, :, :, REC_Z].add(rec_plane)
            image_sum = image_sum + advanced[0] * advanced[1]
            previous, current = current, advanced
        result = jnp.stack((previous[0], current[0], previous[1], current[1]))
        return result.reshape((4, NX, NY * NZ)), image_sum

    outputs, images = lax.map(one_group, (state, source_x, source_y, wavelet, receiver_x, receiver_y, recorded))
    return outputs, image_prior + jnp.sum(images, axis=0)
```

```python
import functools

import jax
import jax.numpy as jnp
from jax import lax
from jax.experimental import pallas as pl
from jax.experimental.pallas import tpu as pltpu
from jax.sharding import PartitionSpec as P

SRC_Z = 4
REC_Z = 2


STENCIL = (-205.0 / 72.0, 8.0 / 5.0, -1.0 / 5.0, 8.0 / 315.0, -1.0 / 560.0)

LANES = 128
ROWS = 16
DEPTH = 64
PER_SHOT = 8
UNROLL = 4
VMEM_BYTES = 48 * 1024 * 1024
MESH = pl.DeviceIdType.MESH


def padded_2(cells, sides, width):
    for axis, dim in sides:
        count = lax.axis_size(axis)
        ends = count - 1
        head = lax.slice_in_dim(cells, 0, width, axis=dim)
        tail = lax.slice_in_dim(cells, cells.shape[dim] - width, cells.shape[dim], axis=dim)
        cells = jnp.concatenate(
            [
                lax.ppermute(tail, axis, [(i, (i + 1) % count) for i in range(ends)]),
                cells,
                lax.ppermute(head, axis, [((i + 1) % count, i) for i in range(ends)]),
            ],
            axis=dim,
        )
    return cells


def laplace(extended):
    width_x = extended.shape[1] - 8
    width_y = extended.shape[2] - 8
    depth = extended.shape[3]
    padded = jnp.pad(extended, ((0, 0), (0, 0), (0, 0), (4, 4)))

    def shifted(dx, dy, dz):
        return padded[
            :, 4 + dx : 4 + dx + width_x, 4 + dy : 4 + dy + width_y, 4 + dz : 4 + dz + depth
        ]

    summed = 3.0 * STENCIL[0] * shifted(0, 0, 0)
    for offset in range(1, 5):
        summed = summed + STENCIL[offset] * (
            shifted(offset, 0, 0)
            + shifted(-offset, 0, 0)
            + shifted(0, offset, 0)
            + shifted(0, -offset, 0)
            + shifted(0, 0, offset)
            + shifted(0, 0, -offset)
        )
    return summed


def inject_sources(
    advanced, x_coords, y_coords, source_x, source_y, wave_value, receiver_x, receiver_y, data_row
):
    src_plane = ((x_coords == source_x[0])[:, None] & (y_coords == source_y[0])[None, :]).astype(
        jnp.float32
    ) * wave_value
    onehot_x = (x_coords[:, None] == receiver_x[0][None, :]).astype(jnp.float32)
    onehot_y = (receiver_y[0][:, None] == y_coords[None, :]).astype(jnp.float32) * data_row[:, None]
    rec_plane = jnp.dot(
        onehot_x, onehot_y, precision=lax.Precision.HIGHEST, preferred_element_type=jnp.float32
    )
    advanced = advanced.at[0, :, :, SRC_Z].add(src_plane)
    return advanced.at[1, :, :, REC_Z].add(rec_plane)


def general_body(
    state, velocity, image_prior, source_x, source_y, wavelet, receiver_x, receiver_y, recorded
):
    step_count = wavelet.shape[1]
    width_x = velocity.shape[0]
    width_y = velocity.shape[1]
    velocity_full = lax.all_gather(velocity, "shot", axis=2, tiled=True)
    depth = velocity_full.shape[2]
    fields = state[0].reshape((4, width_x, width_y, depth))
    previous = jnp.stack((fields[0], fields[2]))
    current = jnp.stack((fields[1], fields[3]))
    base_x = lax.axis_index("gx") * width_x
    base_y = lax.axis_index("gy") * width_y
    image_sum = jnp.zeros(velocity_full.shape, jnp.float32)
    x_coords = base_x + jnp.arange(width_x, dtype=jnp.int32)
    y_coords = base_y + jnp.arange(width_y, dtype=jnp.int32)
    for step_index in range(step_count):
        extended = padded_2(current, (("gx", 1), ("gy", 2)), 4)
        advanced = 2.0 * current - previous + velocity_full[None] * laplace(extended)
        advanced = inject_sources(
            advanced,
            x_coords,
            y_coords,
            source_x,
            source_y,
            wavelet[0, step_index],
            receiver_x,
            receiver_y,
            recorded[0, step_index],
        )
        image_sum = image_sum + advanced[0] * advanced[1]
        previous, current = (current, advanced)
    result = jnp.stack((previous[0], current[0], previous[1], current[1]))
    result = result.reshape((1, 4, width_x, width_y * depth))
    image = image_prior + lax.psum_scatter(image_sum, "shot", scatter_dimension=2, tiled=True)
    return (result, image)


def iota(shape, dim):
    return lax.broadcasted_iota(jnp.int32, shape, dim)


def swap_shot_and_lane(tiles):
    lane = iota(tiles[0].shape, 1)
    for bit in range(3):
        span = 8 << bit
        low = (lane & span) == 0
        new = list(tiles)
        for i in range(8):
            if i & (1 << bit):
                continue
            a, b = tiles[i], tiles[i | (1 << bit)]
            new[i] = jnp.where(low, a, pltpu.roll(b, span, 1))
            new[i | (1 << bit)] = jnp.where(low, pltpu.roll(a, LANES - span, 1), b)
        tiles = new
    return tiles


def thirds(value):
    first = value.astype(jnp.bfloat16)
    rest = value - first.astype(jnp.float32)
    second = rest.astype(jnp.bfloat16)
    return first, second, (rest - second.astype(jnp.float32)).astype(jnp.bfloat16)


def kernel(
    tiles,
    shots,
    sx_hbm,
    sy_hbm,
    wave_hbm,
    st_hbm,
    vel_hbm,
    prior_hbm,
    rx_hbm,
    ry_hbm,
    data_hbm,
    ext,
    last,
    img,
    sx_ref,
    sy_ref,
    wave_ref,
    rx_ref,
    ry_ref,
    data_ref,
    vel_ref,
    prior_ref,
    prev,
    lap,
    vsend,
    vgot,
    vfull,
    inj,
    xsend,
    xgot,
    ysend,
    ygot,
    isum,
    isend,
    igot,
    in_sem,
    xs_sem,
    xr_sem,
    ys_sem,
    yr_sem,
    vs_sem,
    vr_sem,
    is_sem,
    ir_sem,
):
    me = lax.axis_index("shot")
    gx = lax.axis_index("gx")
    gy = lax.axis_index("gy")
    width_y = tiles * LANES // DEPTH
    wide = tiles * LANES
    edge = 2 * LANES
    groups = tiles // 8
    c0, c1, c2, c3, c4 = STENCIL
    coefs = STENCIL
    mids = slice(8, 8 + ROWS)

    barrier = pltpu.get_barrier_semaphore()

    def shot_at(d):
        return lax.rem(me + d, shots)

    for d in range(1, shots):
        pl.semaphore_signal(
            barrier, inc=1, device_id=(shot_at(d), gx, gy), device_id_type=MESH
        )
    pl.semaphore_signal(barrier, inc=1, device_id=(me, 1 - gx, gy), device_id_type=MESH)
    pl.semaphore_signal(barrier, inc=1, device_id=(me, gx, 1 - gy), device_id_type=MESH)

    inner = (pl.ds(8, ROWS), pl.ds(edge, wide))
    firsts = (8 * (1 - gx), 8 * gx)

    def half_rows(half, ahead=0):
        return pl.ds(pl.multiple_of(firsts[half] + ahead, 8), 8)

    moves = [
        (vel_hbm, vel_ref),
        (st_hbm.at[1], ext.at[(0, 0) + inner]),
        (st_hbm.at[3], ext.at[(0, 1) + inner]),
        (rx_hbm, rx_ref),
        (ry_hbm, ry_ref),
        (data_hbm, data_ref),
        (st_hbm.at[0], prev.at[0]),
        (st_hbm.at[2], prev.at[1]),
        (sx_hbm, sx_ref),
        (sy_hbm, sy_ref),
        (wave_hbm, wave_ref),
        (prior_hbm, prior_ref),
    ]
    loads = [pltpu.make_async_copy(a, b, in_sem.at[i]) for i, (a, b) in enumerate(moves)]
    for load in loads:
        load.start()

    def at(t):
        return pl.ds(pl.multiple_of(t * LANES, LANES), LANES)

    for step in range(2):
        for f in range(2):
            for rows in (slice(0, 8), slice(8 + ROWS, 16 + ROWS)):
                ext[step, f, rows, :] = jnp.zeros((8, wide + 2 * edge), jnp.float32)
            for cols in (slice(0, edge), slice(wide + edge, wide + 2 * edge)):
                ext[step, f, mids, cols] = jnp.zeros((ROWS, edge), jnp.float32)

    spot = iota((width_y, groups * LANES), 1)
    in_tile = spot & (LANES - 1)
    y_of = (spot >> 7) * 16 + ((in_tile >> 3) & 7) * 2 + (in_tile >> 6)
    picks = (iota((width_y, groups * LANES), 0) == y_of).astype(jnp.bfloat16)
    own_z = iota((LANES, groups * LANES), 0) & 7
    keep = own_z == (iota((LANES, groups * LANES), 1) & 7)

    loads[0].wait()
    flat = jnp.concatenate(thirds(vel_ref[...].reshape((ROWS * PER_SHOT, width_y))), axis=0)
    spread = jnp.dot(flat, picks, preferred_element_type=jnp.float32)
    rows8 = ROWS * PER_SHOT
    spread = spread[:rows8] + spread[rows8 : 2 * rows8] + spread[2 * rows8 :]
    spread = jnp.where(keep, spread, 0.0).reshape((ROWS, PER_SHOT, groups * LANES))
    packed = jnp.sum(spread, axis=1)
    halves = (
        jnp.where(gx == 0, packed[8:], packed[:8]),
        jnp.where(gx == 0, packed[:8], packed[8:]),
    )
    for half in range(2):
        for u in range(groups):
            vsend[half, u] = halves[half][:, u * LANES : (u + 1) * LANES]
            vgot[me, half, u] = halves[half][:, u * LANES : (u + 1) * LANES]

    top = iota((8, wide), 0) < 4

    def pack_x(step):
        cols = slice(edge, edge + wide)
        p, q = (ext[step, f, half_rows(0, 8), cols] for f in range(2))
        tail = jnp.where(top, pltpu.roll(p, 4, 0), q)
        head = jnp.where(top, p, pltpu.roll(q, 4, 0))
        xsend[step] = jnp.where(gx == 0, tail, head)

    def pack_y(step):
        for f in range(2):
            ysend[step, f] = jnp.where(
                gy == 0,
                ext[step, f, mids, wide : wide + edge],
                ext[step, f, mids, edge : 2 * edge],
            )

    def x_copy(step):
        return pltpu.make_async_remote_copy(
            src_ref=xsend.at[step],
            dst_ref=xgot.at[step],
            send_sem=xs_sem.at[step],
            recv_sem=xr_sem.at[step],
            device_id=(me, 1 - gx, gy),
            device_id_type=MESH,
        )

    def y_copy(step):
        return pltpu.make_async_remote_copy(
            src_ref=ysend.at[step],
            dst_ref=ygot.at[step],
            send_sem=ys_sem.at[step],
            recv_sem=yr_sem.at[step],
            device_id=(me, gx, 1 - gy),
            device_id_type=MESH,
        )

    loads[1].wait()
    loads[2].wait()
    pack_x(0)
    pack_y(0)
    pl.semaphore_wait(barrier, shots + 1)
    vcopies = []
    for half in range(2):
        for d in range(1, shots):
            copy = pltpu.make_async_remote_copy(
                src_ref=vsend.at[half],
                dst_ref=vgot.at[me, half],
                send_sem=vs_sem.at[half, d],
                recv_sem=vr_sem.at[half, d],
                device_id=(shot_at(d), gx, gy),
                device_id_type=MESH,
            )
            copy.start()
            vcopies.append(copy)
        if half == 0:
            xc, yc = x_copy(0), y_copy(0)
            yc.start()
            xc.start()

    lane = iota((ROWS, LANES), 1)
    depth_at = lane & (DEPTH - 1)
    zero = jnp.zeros((ROWS, LANES), jnp.float32)
    base_x = gx * ROWS
    base_y = gy * width_y

    def laplace_own(step):
        def one(quad, carry):
            for part in range(UNROLL):
                t = quad * UNROLL + part
                for f in range(2):
                    near = [ext[step, f, mids, at(t + 2 + k)] for k in (-2, -1, 0, 1, 2)]
                    mid = near[2]
                    total = (3.0 * c0) * mid
                    for k in range(1, 5):
                        total = total + jnp.where(depth_at >= k, coefs[k], 0.0) * pltpu.roll(
                            mid, k, 1
                        )
                        total = total + jnp.where(
                            depth_at < DEPTH - k, coefs[k], 0.0
                        ) * pltpu.roll(mid, LANES - k, 1)
                        total = total + coefs[k] * (
                            ext[step, f, 8 + k : 8 + k + ROWS, at(t + 2)]
                            + ext[step, f, 8 - k : 8 - k + ROWS, at(t + 2)]
                        )
                    total = total + c2 * (near[1] + near[3]) + c4 * (near[0] + near[4])
                    after = c1 * (near[3] + near[2]) + c3 * (near[4] + near[1])
                    before = c1 * (near[2] + near[1]) + c3 * (near[3] + near[0])
                    total = total + pltpu.roll(jnp.where(lane < DEPTH, after, before), DEPTH, 1)
                    lap[f, :, at(t)] = total
            return carry

        lax.fori_loop(0, tiles // UNROLL, one, 0)

    def add_y(step):
        on_left = gy == 1
        on_right = gy == 0
        first = lane < DEPTH
        for f in range(2):
            h0 = ygot[step, f, :, 0:LANES]
            h1 = ygot[step, f, :, LANES:edge]
            a0, a1 = jnp.where(on_left, h0, zero), jnp.where(on_left, h1, zero)
            b0, b1 = jnp.where(on_right, h0, zero), jnp.where(on_right, h1, zero)
            last = tiles - 1
            terms = {
                0: (c2 * a1 + c4 * a0, c3 * a1, c1 * a1 + c3 * a0),
                1: (c4 * a1, zero, c3 * a1),
                last - 1: (c4 * b0, c3 * b0, zero),
                last: (c2 * b0 + c4 * b1, c1 * b0 + c3 * b1, c3 * b0),
            }
            for t, (even, after, before) in terms.items():
                cols = slice(t * LANES, (t + 1) * LANES)
                lap[f, :, cols] = (
                    lap[f, :, cols]
                    + even
                    + pltpu.roll(jnp.where(first, after, before), DEPTH, 1)
                )

    row8 = iota((8, LANES), 0)
    row4 = row8 & 3
    low4 = row8 < 4

    def x_terms(h):
        left = jnp.where(gx == 1, coefs[4], 0.0) * h
        right = jnp.where(gx == 0, coefs[4], 0.0) * h
        for j in range(1, 4):
            left = left + jnp.where((row4 + j < 4) & (gx == 1), coefs[4 - j], 0.0) * pltpu.roll(
                h, 8 - j, 0
            )
            right = right + jnp.where((row4 >= j) & (gx == 0), coefs[4 - j], 0.0) * pltpu.roll(
                h, j, 0
            )
        source = jnp.where(low4, left, pltpu.roll(right, 4, 0))
        receiver = jnp.where(low4, pltpu.roll(left, 4, 0), right)
        return source, receiver

    def advance(step, half):
        wave = wave_ref[0, step]
        rows = half_rows(half)
        inside = half_rows(half, 8)
        source_row = row8 == sx_ref[0] - base_x - firsts[half]

        def one(quad, carry):
            for part in range(UNROLL):
                t = quad * UNROLL + part
                terms = x_terms(xgot[step, :, at(t)]) if half == 0 else None
                v = vfull[half, :, at(t)]
                results = []
                for f in range(2):
                    current = ext[step, f, inside, at(t + 2)]
                    if step == 0:
                        previous = prev[f, rows, at(t)]
                    else:
                        previous = ext[0, f, inside, at(t + 2)]
                    spread_out = lap[f, rows, at(t)]
                    if half == 0:
                        spread_out = spread_out + terms[f]
                    new = 2.0 * current - previous + v * spread_out
                    if f == 0:
                        new = new + jnp.where(
                            source_row & (source_lane + t * LANES == 0), wave, 0.0
                        )
                    else:
                        new = new + inj[step, rows, at(t)]
                    if step == 0:
                        ext[1, f, inside, at(t + 2)] = new
                    else:
                        last[f, rows, at(t)] = new
                    results.append(new)
                product = results[0] * results[1]
                if step == 0:
                    isum[half, :, at(t)] = product
                else:
                    isum[half, :, at(t)] = isum[half, :, at(t)] + product
            return carry

        lax.fori_loop(0, tiles // UNROLL, one, 0)

    for load in loads[3:6]:
        load.wait()
    hit_x = (iota((ROWS, rx_ref.shape[1]), 0) == rx_ref[...] - base_x).astype(jnp.bfloat16)
    hit_y = (iota((width_y, ry_ref.shape[1]), 0) == ry_ref[...] - base_y).astype(jnp.bfloat16)
    parts = []
    for step in range(2):
        parts += [hit_x * piece for piece in thirds(data_ref[step : step + 1, :])]
    planes = lax.dot_general(
        jnp.concatenate(parts, axis=0),
        hit_y,
        (((1,), (1,)), ((), ())),
        preferred_element_type=jnp.float32,
    )
    for step in range(2):
        base = 3 * ROWS * step
        plane = (
            planes[base : base + ROWS]
            + planes[base + ROWS : base + 2 * ROWS]
            + planes[base + 2 * ROWS : base + 3 * ROWS]
        )
        for t in range(tiles):
            even = jnp.broadcast_to(plane[:, 2 * t : 2 * t + 1], (ROWS, LANES))
            odd = jnp.broadcast_to(plane[:, 2 * t + 1 : 2 * t + 2], (ROWS, LANES))
            inj[step, :, t * LANES : (t + 1) * LANES] = jnp.where(
                lane == REC_Z, even, jnp.where(lane == DEPTH + REC_Z, odd, 0.0)
            )

    laplace_own(0)
    for load in loads[6:]:
        load.wait()
    source_lane = iota((8, LANES), 1) - ((sy_ref[0] - base_y) * DEPTH + SRC_Z)
    yc.wait()
    add_y(0)
    next_x = x_copy(1)
    for half in range(2):
        for copy in vcopies[half * (shots - 1) : (half + 1) * (shots - 1)]:
            copy.wait()
        for u in range(groups):
            mixed = swap_shot_and_lane([vgot[s, half, u] for s in range(shots)])
            for i in range(8):
                t = 8 * u + i
                vfull[half, :, t * LANES : (t + 1) * LANES] = mixed[i]
        if half == 0:
            xc.wait()
        advance(0, half)
        if half == 0:
            pack_x(1)
            next_x.start()
    pack_y(1)
    yc = y_copy(1)
    yc.start()

    laplace_own(1)
    yc.wait()
    add_y(1)
    icopies = []
    for half in (1, 0):
        if half == 0:
            next_x.wait()
        advance(1, half)
        for u in range(groups):
            mixed = swap_shot_and_lane(
                [isum[half, :, (8 * u + i) * LANES : (8 * u + i + 1) * LANES] for i in range(8)]
            )
            for s in range(shots):
                isend[half, s, u] = mixed[s]
        for d in range(1, shots):
            to = shot_at(d)
            copy = pltpu.make_async_remote_copy(
                src_ref=isend.at[half, to],
                dst_ref=igot.at[half, d],
                send_sem=is_sem.at[half, d],
                recv_sem=ir_sem.at[half, d],
                device_id=(to, gx, gy),
                device_id_type=MESH,
            )
            copy.start()
            icopies.append(copy)
    image = prior_ref[...].reshape((rows8, width_y))
    sums = [isend[half, me] for half in range(2)]
    for i, half in enumerate((1, 0)):
        for d in range(1, shots):
            icopies[i * (shots - 1) + d - 1].wait()
            sums[half] = sums[half] + igot[half, d]
    for u in range(groups):
        total = jnp.concatenate(
            [
                jnp.where(gx == 0, sums[1][u], sums[0][u]),
                jnp.where(gx == 0, sums[0][u], sums[1][u]),
            ],
            axis=0,
        )
        cols = slice(u * LANES, (u + 1) * LANES)
        tall = jnp.broadcast_to(total[:, None, :], (ROWS, PER_SHOT, LANES))
        tall = jnp.where(keep[:, cols], tall.reshape((rows8, LANES)), 0.0)
        sides = lax.dot_general(
            jnp.concatenate(thirds(tall), axis=0),
            picks[:, cols],
            (((1,), (1,)), ((), ())),
            preferred_element_type=jnp.float32,
        )
        image = image + (sides[:rows8] + sides[rows8 : 2 * rows8] + sides[2 * rows8 :])
    img[...] = image.reshape((ROWS, PER_SHOT, width_y))


def store_kernel(ext, last, img, state_out, image_out, out_sem):
    wide = last.shape[2]
    inner = (pl.ds(8, ROWS), pl.ds(2 * LANES, wide))
    moves = [(img, image_out)]
    for f in range(2):
        moves.append((ext.at[(1, f) + inner], state_out.at[2 * f]))
        moves.append((last.at[f], state_out.at[2 * f + 1]))
    stores = [pltpu.make_async_copy(a, b, out_sem.at[i]) for i, (a, b) in enumerate(moves)]
    for store in stores:
        store.start()
    for store in stores:
        store.wait()


def fast_body(
    state, velocity, image_prior, source_x, source_y, wavelet, receiver_x, receiver_y, recorded
):
    shots = lax.axis_size("shot")
    width_y = velocity.shape[1]
    wide = state.shape[3]
    tiles = wide // LANES
    groups = tiles // 8
    count = receiver_x.shape[1]
    f32 = jnp.float32
    hbm = pl.BlockSpec(memory_space=pltpu.HBM)
    dma = pltpu.SemaphoreType.DMA
    edge = 2 * LANES
    vmem = pl.BlockSpec(memory_space=pltpu.VMEM)
    held = (
        ((2, 2, ROWS + 16, wide + 2 * edge), f32),
        ((2, ROWS, wide), f32),
        ((ROWS, PER_SHOT, width_y), f32),
    )
    pin = lambda a: pltpu.with_memory_space_constraint(a, pltpu.HBM)
    fields = pl.pallas_call(
        functools.partial(kernel, tiles, shots),
        out_shape=tuple(pltpu.VMEM(*a) for a in held),
        in_specs=[hbm] * 9,
        out_specs=(vmem,) * 3,
        scratch_shapes=[
            pltpu.SMEM((1,), jnp.int32),
            pltpu.SMEM((1,), jnp.int32),
            pltpu.SMEM((1, 2), f32),
            pltpu.VMEM((1, count), jnp.int32),
            pltpu.VMEM((1, count), jnp.int32),
            pltpu.VMEM((2, count), f32),
            pltpu.VMEM((ROWS, PER_SHOT, width_y), f32),
            pltpu.VMEM((ROWS, PER_SHOT, width_y), f32),
            pltpu.VMEM((2, ROWS, wide), f32),
            pltpu.VMEM((2, ROWS, wide), f32),
            pltpu.VMEM((2, groups, 8, LANES), f32),
            pltpu.VMEM((shots, 2, groups, 8, LANES), f32),
            pltpu.VMEM((2, 8, wide), f32),
            pltpu.VMEM((2, ROWS, wide), f32),
            pltpu.VMEM((2, 8, wide), f32),
            pltpu.VMEM((2, 8, wide), f32),
            pltpu.VMEM((2, 2, ROWS, edge), f32),
            pltpu.VMEM((2, 2, ROWS, edge), f32),
            pltpu.VMEM((2, 8, wide), f32),
            pltpu.VMEM((2, shots, groups, 8, LANES), f32),
            pltpu.VMEM((2, shots, groups, 8, LANES), f32),
            dma((12,)),
            dma((2,)),
            dma((2,)),
            dma((2,)),
            dma((2,)),
            dma((2, shots)),
            dma((2, shots)),
            dma((2, shots)),
            dma((2, shots)),
        ],
        compiler_params=pltpu.CompilerParams(
            collective_id=0, has_side_effects=True, vmem_limit_bytes=VMEM_BYTES
        ),
    )(
        source_x,
        source_y,
        pin(wavelet),
        pin(state[0]),
        pin(jnp.swapaxes(velocity, 1, 2)),
        pin(jnp.swapaxes(image_prior, 1, 2)),
        pin(receiver_x),
        pin(receiver_y),
        pin(recorded[0]),
    )
    fields = [pltpu.with_memory_space_constraint(a, pltpu.VMEM) for a in fields]
    out, img = pl.pallas_call(
        store_kernel,
        out_shape=(
            jax.ShapeDtypeStruct((4, ROWS, wide), f32),
            jax.ShapeDtypeStruct((ROWS, PER_SHOT, width_y), f32),
        ),
        in_specs=[vmem] * 3,
        out_specs=(hbm, hbm),
        scratch_shapes=[dma((5,))],
        compiler_params=pltpu.CompilerParams(vmem_limit_bytes=VMEM_BYTES),
    )(*fields)
    return (out[None], jnp.swapaxes(img, 1, 2))


def body(
    state, velocity, image_prior, source_x, source_y, wavelet, receiver_x, receiver_y, recorded
):
    shots = lax.axis_size("shot")
    width_x, width_y, per_shot = velocity.shape
    fits = (
        shots == 8
        and lax.axis_size("gx") == 2
        and lax.axis_size("gy") == 2
        and per_shot == PER_SHOT
        and width_x == ROWS
        and width_y % 16 == 0
        and wavelet.shape[1] == 2
    )
    chosen = fast_body if fits else general_body
    return chosen(
        state, velocity, image_prior, source_x, source_y, wavelet, receiver_x, receiver_y, recorded
    )


def solution(mesh):
    in_specs = (
        P("shot", None, "gx", "gy"),
        P("gx", "gy", "shot"),
        P("gx", "gy", "shot"),
        P("shot"),
        P("shot"),
        P("shot", None),
        P("shot", None),
        P("shot", None),
        P("shot", None, None),
    )
    out_specs = (P("shot", None, "gx", "gy"), P("gx", "gy", "shot"))
    return jax.shard_map(body, mesh=mesh, in_specs=in_specs, out_specs=out_specs, check_vma=False)
```

```python
import functools

import jax
import jax.numpy as jnp
from jax import lax
from jax.experimental import pallas as pl
from jax.experimental.pallas import tpu as pltpu
from jax.sharding import PartitionSpec as P

SRC_Z = 4
REC_Z = 2


STENCIL = (-205.0 / 72.0, 8.0 / 5.0, -1.0 / 5.0, 8.0 / 315.0, -1.0 / 560.0)

LANES = 128
ROWS = 16
DEPTH = 64
PER_SHOT = 8
UNROLL = 4
VMEM_BYTES = 48 * 1024 * 1024
MESH = pl.DeviceIdType.MESH
IMAGE_PARTS = ((1, 1, 1, 1), (1, 0, 1, 0), (0, 0, 1, 0), (1, 2, 1, 2), (0, 1, 1, 1), (0, 2, 1, 2))
VEL_PARTS = ((0, 0, 1), (0, 1, 1), (0, 2, 1), (1, 0, 1), (1, 1, 1), (1, 2, 1))


def padded_2(cells, sides, width):
    for axis, dim in sides:
        count = lax.axis_size(axis)
        ends = count - 1
        head = lax.slice_in_dim(cells, 0, width, axis=dim)
        tail = lax.slice_in_dim(cells, cells.shape[dim] - width, cells.shape[dim], axis=dim)
        cells = jnp.concatenate(
            [
                lax.ppermute(tail, axis, [(i, (i + 1) % count) for i in range(ends)]),
                cells,
                lax.ppermute(head, axis, [((i + 1) % count, i) for i in range(ends)]),
            ],
            axis=dim,
        )
    return cells


def laplace(extended):
    width_x = extended.shape[1] - 8
    width_y = extended.shape[2] - 8
    depth = extended.shape[3]
    padded = jnp.pad(extended, ((0, 0), (0, 0), (0, 0), (4, 4)))

    def shifted(dx, dy, dz):
        return padded[
            :, 4 + dx : 4 + dx + width_x, 4 + dy : 4 + dy + width_y, 4 + dz : 4 + dz + depth
        ]

    summed = 3.0 * STENCIL[0] * shifted(0, 0, 0)
    for offset in range(1, 5):
        summed = summed + STENCIL[offset] * (
            shifted(offset, 0, 0)
            + shifted(-offset, 0, 0)
            + shifted(0, offset, 0)
            + shifted(0, -offset, 0)
            + shifted(0, 0, offset)
            + shifted(0, 0, -offset)
        )
    return summed


def inject_sources(
    advanced, x_coords, y_coords, source_x, source_y, wave_value, receiver_x, receiver_y, data_row
):
    src_plane = ((x_coords == source_x[0])[:, None] & (y_coords == source_y[0])[None, :]).astype(
        jnp.float32
    ) * wave_value
    onehot_x = (x_coords[:, None] == receiver_x[0][None, :]).astype(jnp.float32)
    onehot_y = (receiver_y[0][:, None] == y_coords[None, :]).astype(jnp.float32) * data_row[:, None]
    rec_plane = jnp.dot(
        onehot_x, onehot_y, precision=lax.Precision.HIGHEST, preferred_element_type=jnp.float32
    )
    advanced = advanced.at[0, :, :, SRC_Z].add(src_plane)
    return advanced.at[1, :, :, REC_Z].add(rec_plane)


def general_body(
    state, velocity, image_prior, source_x, source_y, wavelet, receiver_x, receiver_y, recorded
):
    step_count = wavelet.shape[1]
    width_x = velocity.shape[0]
    width_y = velocity.shape[1]
    velocity_full = lax.all_gather(velocity, "shot", axis=2, tiled=True)
    depth = velocity_full.shape[2]
    fields = state[0].reshape((4, width_x, width_y, depth))
    previous = jnp.stack((fields[0], fields[2]))
    current = jnp.stack((fields[1], fields[3]))
    base_x = lax.axis_index("gx") * width_x
    base_y = lax.axis_index("gy") * width_y
    image_sum = jnp.zeros(velocity_full.shape, jnp.float32)
    x_coords = base_x + jnp.arange(width_x, dtype=jnp.int32)
    y_coords = base_y + jnp.arange(width_y, dtype=jnp.int32)
    for step_index in range(step_count):
        extended = padded_2(current, (("gx", 1), ("gy", 2)), 4)
        advanced = 2.0 * current - previous + velocity_full[None] * laplace(extended)
        advanced = inject_sources(
            advanced,
            x_coords,
            y_coords,
            source_x,
            source_y,
            wavelet[0, step_index],
            receiver_x,
            receiver_y,
            recorded[0, step_index],
        )
        image_sum = image_sum + advanced[0] * advanced[1]
        previous, current = (current, advanced)
    result = jnp.stack((previous[0], current[0], previous[1], current[1]))
    result = result.reshape((1, 4, width_x, width_y * depth))
    image = image_prior + lax.psum_scatter(image_sum, "shot", scatter_dimension=2, tiled=True)
    return (result, image)


def iota(shape, dim):
    return lax.broadcasted_iota(jnp.int32, shape, dim)


def swap_shot_and_lane(tiles):
    lane = iota(tiles[0].shape, 1)
    for bit in range(3):
        span = 8 << bit
        low = (lane & span) == 0
        new = list(tiles)
        for i in range(8):
            if i & (1 << bit):
                continue
            a, b = tiles[i], tiles[i | (1 << bit)]
            new[i] = jnp.where(low, a, pltpu.roll(b, span, 1))
            new[i | (1 << bit)] = jnp.where(low, pltpu.roll(a, LANES - span, 1), b)
        tiles = new
    return tiles


def pieces(value):
    first = value.astype(jnp.bfloat16)
    return first, (value - first.astype(jnp.float32)).astype(jnp.bfloat16)


def depth_picks(groups, width_y):
    spot = iota((width_y, groups * LANES), 1)
    in_tile = spot & (LANES - 1)
    y_of = (spot >> 7) * 16 + ((in_tile >> 3) & 7) * 2 + (in_tile >> 6)
    picks = (iota((width_y, groups * LANES), 0) == y_of).astype(jnp.bfloat16)
    own_z = iota((LANES, groups * LANES), 0) & 7
    keep = own_z == (iota((LANES, groups * LANES), 1) & 7)
    return picks, keep


def thirds(value):
    first = value.astype(jnp.bfloat16)
    rest = value - first.astype(jnp.float32)
    second = rest.astype(jnp.bfloat16)
    return first, second, (rest - second.astype(jnp.float32)).astype(jnp.bfloat16)


def kernel(
    tiles,
    shots,
    sx_hbm,
    sy_hbm,
    wave_hbm,
    st_hbm,
    vel_hbm,
    prior_hbm,
    rx_hbm,
    ry_hbm,
    data_hbm,
    ext,
    last,
    total,
    prior_ref,
    sx_ref,
    sy_ref,
    wave_ref,
    rx_ref,
    ry_ref,
    data_ref,
    vel_ref,
    prev,
    lap,
    vgot,
    vfull,
    inj,
    xsend,
    xgot,
    ysend,
    ygot,
    isum,
    isend,
    igot,
    in_sem,
    xs_sem,
    xr_sem,
    ys_sem,
    yr_sem,
    vs_sem,
    vr_sem,
    is_sem,
    ir_sem,
):
    me = lax.axis_index("shot")
    gx = lax.axis_index("gx")
    gy = lax.axis_index("gy")
    width_y = tiles * LANES // DEPTH
    wide = tiles * LANES
    edge = 2 * LANES
    groups = tiles // 8
    c0, c1, c2, c3, c4 = STENCIL
    coefs = STENCIL
    mids = slice(8, 8 + ROWS)

    barrier = pltpu.get_barrier_semaphore()

    def shot_at(d):
        return sum(lax.rem(me // bit + d // bit, 2) * bit for bit in (1, 2, 4))

    def group_at(k):
        return k * gy + (groups - 1 - k) * (1 - gy)

    def in_order(values):
        return [jnp.where(gy == 1, values[k], values[groups - 1 - k]) for k in range(groups)]

    for d in range(1, shots):
        pl.semaphore_signal(
            barrier, inc=1, device_id=(shot_at(d), gx, gy), device_id_type=MESH
        )
    pl.semaphore_signal(barrier, inc=1, device_id=(me, 1 - gx, gy), device_id_type=MESH)
    pl.semaphore_signal(barrier, inc=1, device_id=(me, gx, 1 - gy), device_id_type=MESH)

    inner = (pl.ds(8, ROWS), pl.ds(edge, wide))
    firsts = (8 * (1 - gx), 8 * gx)

    def half_rows(half, ahead=0):
        return pl.ds(pl.multiple_of(firsts[half] + ahead, 8), 8)

    moves = [
        (vel_hbm, vel_ref),
        (st_hbm.at[1], ext.at[(0, 0) + inner]),
        (st_hbm.at[3], ext.at[(0, 1) + inner]),
        (rx_hbm, rx_ref),
        (ry_hbm, ry_ref),
        (data_hbm, data_ref),
        (st_hbm.at[0], prev.at[0]),
        (st_hbm.at[2], prev.at[1]),
        (sx_hbm, sx_ref),
        (sy_hbm, sy_ref),
        (wave_hbm, wave_ref),
        (prior_hbm, prior_ref),
    ]
    loads = [pltpu.make_async_copy(a, b, in_sem.at[i]) for i, (a, b) in enumerate(moves)]
    for load in loads:
        load.start()

    def at(t):
        return pl.ds(pl.multiple_of(t * LANES, LANES), LANES)

    for step in range(2):
        for f in range(2):
            for rows in (slice(0, 8), slice(8 + ROWS, 16 + ROWS)):
                ext[step, f, rows, :] = jnp.zeros((8, wide + 2 * edge), jnp.float32)
            for cols in (slice(0, edge), slice(wide + edge, wide + 2 * edge)):
                ext[step, f, mids, cols] = jnp.zeros((ROWS, edge), jnp.float32)

    picks, keep = depth_picks(groups, width_y)

    loads[0].wait()
    flat = jnp.concatenate(pieces(vel_ref[...].reshape((ROWS * PER_SHOT, width_y))), axis=0)
    spread = jnp.dot(flat, picks, preferred_element_type=jnp.float32)
    rows8 = ROWS * PER_SHOT
    spread = spread[:rows8] + spread[rows8:]
    spread = jnp.where(keep, spread, 0.0).reshape((ROWS, PER_SHOT, groups * LANES))
    packed = jnp.sum(spread, axis=1)
    halves = (
        jnp.where(gx == 0, packed[8:], packed[:8]),
        jnp.where(gx == 0, packed[:8], packed[8:]),
    )
    for half in range(2):
        mine = [halves[half][:, u * LANES : (u + 1) * LANES] for u in range(groups)]
        for k, tile in enumerate(in_order(mine)):
            vgot[half, 0, k] = tile

    def columns(u):
        return pl.ds(pl.multiple_of(u * 8 * LANES, 8 * LANES), 8 * LANES)

    top = iota((8, 8 * LANES), 0) < 4

    def pack_x(step, u):
        cols = pl.ds(pl.multiple_of(u * 8 * LANES + edge, LANES), 8 * LANES)
        p, q = (ext[step, f, half_rows(0, 8), cols] for f in range(2))
        tail = jnp.where(top, pltpu.roll(p, 4, 0), q)
        head = jnp.where(top, p, pltpu.roll(q, 4, 0))
        xsend[step, :, columns(u)] = jnp.where(gx == 0, tail, head)

    def pack_y(step):
        for f in range(2):
            ysend[step, f] = jnp.where(
                gy == 0,
                ext[step, f, mids, wide : wide + edge],
                ext[step, f, mids, edge : 2 * edge],
            )

    def x_copy(step, k):
        part = (step,) if step == 0 else (step, slice(None), columns(group_at(k)))
        return pltpu.make_async_remote_copy(
            src_ref=xsend.at[part],
            dst_ref=xgot.at[part],
            send_sem=xs_sem.at[step + k],
            recv_sem=xr_sem.at[step + k],
            device_id=(me, 1 - gx, gy),
            device_id_type=MESH,
        )

    def y_copy(step):
        return pltpu.make_async_remote_copy(
            src_ref=ysend.at[step],
            dst_ref=ygot.at[step],
            send_sem=ys_sem.at[step],
            recv_sem=yr_sem.at[step],
            device_id=(me, gx, 1 - gy),
            device_id_type=MESH,
        )

    loads[1].wait()
    loads[2].wait()
    for u in range(groups):
        pack_x(0, u)
    pack_y(0)
    pl.semaphore_wait(barrier, shots + 1)
    xc, yc = x_copy(0, 0), y_copy(0)
    for part, (half, first, count) in enumerate(VEL_PARTS):
        for d in reversed(range(1, shots)):
            pltpu.make_async_remote_copy(
                src_ref=vgot.at[half, 0, pl.ds(first, count)],
                dst_ref=vgot.at[half, d, pl.ds(first, count)],
                send_sem=vs_sem.at[part],
                recv_sem=vr_sem.at[part],
                device_id=(shot_at(d), gx, gy),
                device_id_type=MESH,
            ).start()
        if part == 0:
            yc.start()
            xc.start()

    lane = iota((ROWS, LANES), 1)
    depth_at = lane & (DEPTH - 1)
    zero = jnp.zeros((ROWS, LANES), jnp.float32)
    base_x = gx * ROWS
    base_y = gy * width_y

    def laplace_own(step, first, count):
        def one(quad, carry):
            for part in range(UNROLL):
                t = first + quad * UNROLL + part
                for f in range(2):
                    near = [ext[step, f, mids, at(t + 2 + k)] for k in (-2, -1, 0, 1, 2)]
                    mid = near[2]
                    total = (3.0 * c0) * mid
                    for k in range(1, 5):
                        total = total + jnp.where(depth_at >= k, coefs[k], 0.0) * pltpu.roll(
                            mid, k, 1
                        )
                        total = total + jnp.where(
                            depth_at < DEPTH - k, coefs[k], 0.0
                        ) * pltpu.roll(mid, LANES - k, 1)
                        total = total + coefs[k] * (
                            ext[step, f, 8 + k : 8 + k + ROWS, at(t + 2)]
                            + ext[step, f, 8 - k : 8 - k + ROWS, at(t + 2)]
                        )
                    total = total + c2 * (near[1] + near[3]) + c4 * (near[0] + near[4])
                    after = c1 * (near[3] + near[2]) + c3 * (near[4] + near[1])
                    before = c1 * (near[2] + near[1]) + c3 * (near[3] + near[0])
                    total = total + pltpu.roll(jnp.where(lane < DEPTH, after, before), DEPTH, 1)
                    lap[f, :, at(t)] = total
            return carry

        lax.fori_loop(0, count // UNROLL, one, 0)

    def add_y(step):
        on_left = gy == 1
        on_right = gy == 0
        first = lane < DEPTH
        for f in range(2):
            h0 = ygot[step, f, :, 0:LANES]
            h1 = ygot[step, f, :, LANES:edge]
            a0, a1 = jnp.where(on_left, h0, zero), jnp.where(on_left, h1, zero)
            b0, b1 = jnp.where(on_right, h0, zero), jnp.where(on_right, h1, zero)
            end = tiles - 1
            terms = {
                0: (c2 * a1 + c4 * a0, c3 * a1, c1 * a1 + c3 * a0),
                1: (c4 * a1, zero, c3 * a1),
                end - 1: (c4 * b0, c3 * b0, zero),
                end: (c2 * b0 + c4 * b1, c1 * b0 + c3 * b1, c3 * b0),
            }
            for t, (even, after, before) in terms.items():
                cols = slice(t * LANES, (t + 1) * LANES)
                lap[f, :, cols] = (
                    lap[f, :, cols]
                    + even
                    + pltpu.roll(jnp.where(first, after, before), DEPTH, 1)
                )

    row8 = iota((8, LANES), 0)
    row4 = row8 & 3
    low4 = row8 < 4

    def x_terms(h):
        left = jnp.where(gx == 1, coefs[4], 0.0) * h
        right = jnp.where(gx == 0, coefs[4], 0.0) * h
        for j in range(1, 4):
            left = left + jnp.where((row4 + j < 4) & (gx == 1), coefs[4 - j], 0.0) * pltpu.roll(
                h, 8 - j, 0
            )
            right = right + jnp.where((row4 >= j) & (gx == 0), coefs[4 - j], 0.0) * pltpu.roll(
                h, j, 0
            )
        source = jnp.where(low4, left, pltpu.roll(right, 4, 0))
        receiver = jnp.where(low4, pltpu.roll(left, 4, 0), right)
        return source, receiver

    def advance(step, half, u):
        wave = wave_ref[0, step]
        rows = half_rows(half)
        inside = half_rows(half, 8)
        source_row = row8 == sx_ref[0] - base_x - firsts[half]

        def one(quad, carry):
            for part in range(UNROLL):
                t = u * 8 + quad * UNROLL + part
                terms = x_terms(xgot[step, :, at(t)]) if half == 0 else None
                v = vfull[half, :, at(t)]
                results = []
                for f in range(2):
                    current = ext[step, f, inside, at(t + 2)]
                    if step == 0:
                        previous = prev[f, rows, at(t)]
                    else:
                        previous = ext[0, f, inside, at(t + 2)]
                    spread_out = lap[f, rows, at(t)]
                    if half == 0:
                        spread_out = spread_out + terms[f]
                    new = 2.0 * current - previous + v * spread_out
                    if f == 0:
                        new = new + jnp.where(
                            source_row & (source_lane + t * LANES == 0), wave, 0.0
                        )
                    else:
                        new = new + inj[step, rows, at(t)]
                    if step == 0:
                        ext[1, f, inside, at(t + 2)] = new
                    else:
                        last[f, rows, at(t)] = new
                    results.append(new)
                product = results[0] * results[1]
                if step == 0:
                    isum[half, :, at(t)] = product
                else:
                    isum[half, :, at(t)] = isum[half, :, at(t)] + product
            return carry

        lax.fori_loop(0, 8 // UNROLL, one, 0)

    for load in loads[3:6]:
        load.wait()
    hit_x = (iota((ROWS, rx_ref.shape[1]), 0) == rx_ref[...] - base_x).astype(jnp.bfloat16)
    hit_y = (iota((width_y, ry_ref.shape[1]), 0) == ry_ref[...] - base_y).astype(jnp.bfloat16)
    parts = []
    for step in range(2):
        parts += [hit_x * piece for piece in thirds(data_ref[step : step + 1, :])]
    planes = lax.dot_general(
        jnp.concatenate(parts, axis=0),
        hit_y,
        (((1,), (1,)), ((), ())),
        preferred_element_type=jnp.float32,
    )
    for step in range(2):
        base = 3 * ROWS * step
        plane = (
            planes[base : base + ROWS]
            + planes[base + ROWS : base + 2 * ROWS]
            + planes[base + 2 * ROWS : base + 3 * ROWS]
        )
        for t in range(tiles):
            even = jnp.broadcast_to(plane[:, 2 * t : 2 * t + 1], (ROWS, LANES))
            odd = jnp.broadcast_to(plane[:, 2 * t + 1 : 2 * t + 2], (ROWS, LANES))
            inj[step, :, t * LANES : (t + 1) * LANES] = jnp.where(
                lane == REC_Z, even, jnp.where(lane == DEPTH + REC_Z, odd, 0.0)
            )

    laplace_own(0, 0, tiles)
    for load in loads[6:11]:
        load.wait()
    source_lane = iota((8, LANES), 1) - ((sy_ref[0] - base_y) * DEPTH + SRC_Z)
    yc.wait_recv()
    add_y(0)

    def arrived(ref, sem):
        pltpu.make_async_copy(ref, ref, sem).wait()

    others = pl.ds(1, shots - 1)
    slots = [shot_at(s) for s in range(shots)]
    xcopies = [x_copy(1, k) for k in range(groups)]
    next_y = y_copy(1)

    def send_image(half, k):
        u = group_at(k)
        mixed = swap_shot_and_lane([isum[half, :, at(8 * u + i)] for i in range(8)])
        for s in range(shots):
            isend[half, s, k] = mixed[s]
        for part, (of, first, count, after) in enumerate(IMAGE_PARTS):
            if (of, after) != (half, k):
                continue
            for d in reversed(range(1, shots)):
                to = shot_at(d)
                pltpu.make_async_remote_copy(
                    src_ref=isend.at[half, to, pl.ds(first, count)],
                    dst_ref=igot.at[half, d, pl.ds(first, count)],
                    send_sem=is_sem.at[part],
                    recv_sem=ir_sem.at[part],
                    device_id=(to, gx, gy),
                    device_id_type=MESH,
                ).start()

    def near_half(k):
        xcopies[k].wait_recv()
        advance(1, 0, group_at(k))
        send_image(0, k)

    def far_half(k):
        advance(1, 1, group_at(k))
        send_image(1, k)

    for part, (half, first, count) in enumerate(VEL_PARTS):
        arrived(vgot.at[half, others, pl.ds(first, count)], vr_sem.at[part])
        for k in range(first, first + count):
            u = group_at(k)
            mixed = swap_shot_and_lane([vgot[half, slots[s], k] for s in range(shots)])
            for i in range(8):
                vfull[half, :, at(8 * u + i)] = mixed[i]
            if half == 0 and k == 0:
                xc.wait_recv()
            advance(0, half, u)
            if half == 0:
                pack_x(1, u)
                xcopies[k].start()
                continue
            if k == 0:
                pack_y(1)
                next_y.start()
            else:
                laplace_own(1, 8 * group_at(k - 1), 8)
            if k > 1:
                far_half(k - 1)
    next_y.wait_recv()
    add_y(1)
    far_half(0)
    near_half(0)
    laplace_own(1, 8 * group_at(groups - 1), 8)
    far_half(groups - 1)
    for k in range(1, groups):
        near_half(k)
    for part, (half, first, count) in enumerate(VEL_PARTS):
        arrived(vgot.at[half, others, pl.ds(first, count)], vs_sem.at[part])
    for copy in (xc, yc, next_y, *xcopies):
        copy.wait_send()
    loads[11].wait()
    for part, (half, first, count, _) in enumerate(IMAGE_PARTS):
        arrived(igot.at[half, others, pl.ds(first, count)], ir_sem.at[part])
        for k in range(first, first + count):
            summed = isend[half, me, k]
            for d in range(1, shots):
                summed = summed + igot[half, d, k]
            total[group_at(k), half_rows(half), :] = summed
    for part, (half, first, count, _) in enumerate(IMAGE_PARTS):
        arrived(igot.at[half, others, pl.ds(first, count)], is_sem.at[part])


def store_kernel(ext, last, total, prior, state_out, image_out, img, out_sem):
    wide = last.shape[2]
    groups = total.shape[0]
    width_y = prior.shape[2]
    rows8 = ROWS * PER_SHOT
    inner = (pl.ds(8, ROWS), pl.ds(2 * LANES, wide))
    moves = []
    for f in range(2):
        moves.append((ext.at[(1, f) + inner], state_out.at[2 * f]))
        moves.append((last.at[f], state_out.at[2 * f + 1]))
    moves.append((img, image_out))
    stores = [pltpu.make_async_copy(a, b, out_sem.at[i]) for i, (a, b) in enumerate(moves)]
    for store in stores[:4]:
        store.start()
    picks, keep = depth_picks(groups, width_y)
    image = prior[...].reshape((rows8, width_y))
    for u in range(groups):
        cols = slice(u * LANES, (u + 1) * LANES)
        tall = jnp.broadcast_to(total[u][:, None, :], (ROWS, PER_SHOT, LANES))
        tall = jnp.where(keep[:, cols], tall.reshape((rows8, LANES)), 0.0)
        sides = lax.dot_general(
            jnp.concatenate(pieces(tall), axis=0),
            picks[:, cols],
            (((1,), (1,)), ((), ())),
            preferred_element_type=jnp.float32,
        )
        image = image + (sides[:rows8] + sides[rows8:])
    img[...] = image.reshape((ROWS, PER_SHOT, width_y))
    stores[4].start()
    for store in stores:
        store.wait()


def fast_body(
    state, velocity, image_prior, source_x, source_y, wavelet, receiver_x, receiver_y, recorded
):
    shots = lax.axis_size("shot")
    width_y = velocity.shape[1]
    wide = state.shape[3]
    tiles = wide // LANES
    groups = tiles // 8
    count = receiver_x.shape[1]
    f32 = jnp.float32
    hbm = pl.BlockSpec(memory_space=pltpu.HBM)
    dma = pltpu.SemaphoreType.DMA
    edge = 2 * LANES
    vmem = pl.BlockSpec(memory_space=pltpu.VMEM)
    held = (
        ((2, 2, ROWS + 16, wide + 2 * edge), f32),
        ((2, ROWS, wide), f32),
        ((groups, ROWS, LANES), f32),
        ((ROWS, PER_SHOT, width_y), f32),
    )
    pin = lambda a: pltpu.with_memory_space_constraint(a, pltpu.HBM)
    fields = pl.pallas_call(
        functools.partial(kernel, tiles, shots),
        out_shape=tuple(pltpu.VMEM(*a) for a in held),
        in_specs=[hbm] * 9,
        out_specs=(vmem,) * 4,
        scratch_shapes=[
            pltpu.SMEM((1,), jnp.int32),
            pltpu.SMEM((1,), jnp.int32),
            pltpu.SMEM((1, 2), f32),
            pltpu.VMEM((1, count), jnp.int32),
            pltpu.VMEM((1, count), jnp.int32),
            pltpu.VMEM((2, count), f32),
            pltpu.VMEM((ROWS, PER_SHOT, width_y), f32),
            pltpu.VMEM((2, ROWS, wide), f32),
            pltpu.VMEM((2, ROWS, wide), f32),
            pltpu.VMEM((2, shots, groups, 8, LANES), f32),
            pltpu.VMEM((2, 8, wide), f32),
            pltpu.VMEM((2, ROWS, wide), f32),
            pltpu.VMEM((2, 8, wide), f32),
            pltpu.VMEM((2, 8, wide), f32),
            pltpu.VMEM((2, 2, ROWS, edge), f32),
            pltpu.VMEM((2, 2, ROWS, edge), f32),
            pltpu.VMEM((2, 8, wide), f32),
            pltpu.VMEM((2, shots, groups, 8, LANES), f32),
            pltpu.VMEM((2, shots, groups, 8, LANES), f32),
            dma((12,)),
            dma((1 + groups,)),
            dma((1 + groups,)),
            dma((2,)),
            dma((2,)),
            dma((len(VEL_PARTS),)),
            dma((len(VEL_PARTS),)),
            dma((len(IMAGE_PARTS),)),
            dma((len(IMAGE_PARTS),)),
        ],
        compiler_params=pltpu.CompilerParams(
            collective_id=0, has_side_effects=True, vmem_limit_bytes=VMEM_BYTES
        ),
    )(
        source_x,
        source_y,
        pin(wavelet),
        pin(state[0]),
        pin(jnp.swapaxes(velocity, 1, 2)),
        pin(jnp.swapaxes(image_prior, 1, 2)),
        pin(receiver_x),
        pin(receiver_y),
        pin(recorded[0]),
    )
    fields = [pltpu.with_memory_space_constraint(a, pltpu.VMEM) for a in fields]
    out, img = pl.pallas_call(
        store_kernel,
        out_shape=(
            jax.ShapeDtypeStruct((4, ROWS, wide), f32),
            jax.ShapeDtypeStruct((ROWS, PER_SHOT, width_y), f32),
        ),
        in_specs=[vmem] * 4,
        out_specs=(hbm, hbm),
        scratch_shapes=[pltpu.VMEM((ROWS, PER_SHOT, width_y), f32), dma((5,))],
        compiler_params=pltpu.CompilerParams(vmem_limit_bytes=VMEM_BYTES),
    )(*fields)
    return (out[None], jnp.swapaxes(img, 1, 2))


def body(
    state, velocity, image_prior, source_x, source_y, wavelet, receiver_x, receiver_y, recorded
):
    shots = lax.axis_size("shot")
    width_x, width_y, per_shot = velocity.shape
    fits = (
        shots == 8
        and lax.axis_size("gx") == 2
        and lax.axis_size("gy") == 2
        and per_shot == PER_SHOT
        and width_x == ROWS
        and width_y % 16 == 0
        and wavelet.shape[1] == 2
    )
    chosen = fast_body if fits else general_body
    return chosen(
        state, velocity, image_prior, source_x, source_y, wavelet, receiver_x, receiver_y, recorded
    )


def solution(mesh):
    in_specs = (
        P("shot", None, "gx", "gy"),
        P("gx", "gy", "shot"),
        P("gx", "gy", "shot"),
        P("shot"),
        P("shot"),
        P("shot", None),
        P("shot", None),
        P("shot", None),
        P("shot", None, None),
    )
    out_specs = (P("shot", None, "gx", "gy"), P("gx", "gy", "shot"))
    return jax.shard_map(body, mesh=mesh, in_specs=in_specs, out_specs=out_specs, check_vma=False)
```

```python
import functools

import jax
import jax.numpy as jnp
from jax import lax
from jax.experimental import pallas as pl
from jax.experimental.pallas import tpu as pltpu
from jax.sharding import PartitionSpec as P

SRC_Z = 4
REC_Z = 2


STENCIL = (-205.0 / 72.0, 8.0 / 5.0, -1.0 / 5.0, 8.0 / 315.0, -1.0 / 560.0)

LANES = 128
ROWS = 16
DEPTH = 64
PER_SHOT = 8
UNROLL = 4
VMEM_BYTES = 48 * 1024 * 1024
MESH = pl.DeviceIdType.MESH
VEL_PARTS = ((0, 0), (0, 2), (0, 1), (1, 0), (1, 1), (1, 2))


def padded_2(cells, sides, width):
    for axis, dim in sides:
        count = lax.axis_size(axis)
        ends = count - 1
        head = lax.slice_in_dim(cells, 0, width, axis=dim)
        tail = lax.slice_in_dim(cells, cells.shape[dim] - width, cells.shape[dim], axis=dim)
        cells = jnp.concatenate(
            [
                lax.ppermute(tail, axis, [(i, (i + 1) % count) for i in range(ends)]),
                cells,
                lax.ppermute(head, axis, [((i + 1) % count, i) for i in range(ends)]),
            ],
            axis=dim,
        )
    return cells


def laplace(extended):
    width_x = extended.shape[1] - 8
    width_y = extended.shape[2] - 8
    depth = extended.shape[3]
    padded = jnp.pad(extended, ((0, 0), (0, 0), (0, 0), (4, 4)))

    def shifted(dx, dy, dz):
        return padded[
            :, 4 + dx : 4 + dx + width_x, 4 + dy : 4 + dy + width_y, 4 + dz : 4 + dz + depth
        ]

    summed = 3.0 * STENCIL[0] * shifted(0, 0, 0)
    for offset in range(1, 5):
        summed = summed + STENCIL[offset] * (
            shifted(offset, 0, 0)
            + shifted(-offset, 0, 0)
            + shifted(0, offset, 0)
            + shifted(0, -offset, 0)
            + shifted(0, 0, offset)
            + shifted(0, 0, -offset)
        )
    return summed


def inject_sources(
    advanced, x_coords, y_coords, source_x, source_y, wave_value, receiver_x, receiver_y, data_row
):
    src_plane = ((x_coords == source_x[0])[:, None] & (y_coords == source_y[0])[None, :]).astype(
        jnp.float32
    ) * wave_value
    onehot_x = (x_coords[:, None] == receiver_x[0][None, :]).astype(jnp.float32)
    onehot_y = (receiver_y[0][:, None] == y_coords[None, :]).astype(jnp.float32) * data_row[:, None]
    rec_plane = jnp.dot(
        onehot_x, onehot_y, precision=lax.Precision.HIGHEST, preferred_element_type=jnp.float32
    )
    advanced = advanced.at[0, :, :, SRC_Z].add(src_plane)
    return advanced.at[1, :, :, REC_Z].add(rec_plane)


def general_body(
    state, velocity, image_prior, source_x, source_y, wavelet, receiver_x, receiver_y, recorded
):
    step_count = wavelet.shape[1]
    width_x = velocity.shape[0]
    width_y = velocity.shape[1]
    velocity_full = lax.all_gather(velocity, "shot", axis=2, tiled=True)
    depth = velocity_full.shape[2]
    fields = state[0].reshape((4, width_x, width_y, depth))
    previous = jnp.stack((fields[0], fields[2]))
    current = jnp.stack((fields[1], fields[3]))
    base_x = lax.axis_index("gx") * width_x
    base_y = lax.axis_index("gy") * width_y
    image_sum = jnp.zeros(velocity_full.shape, jnp.float32)
    x_coords = base_x + jnp.arange(width_x, dtype=jnp.int32)
    y_coords = base_y + jnp.arange(width_y, dtype=jnp.int32)
    for step_index in range(step_count):
        extended = padded_2(current, (("gx", 1), ("gy", 2)), 4)
        advanced = 2.0 * current - previous + velocity_full[None] * laplace(extended)
        advanced = inject_sources(
            advanced,
            x_coords,
            y_coords,
            source_x,
            source_y,
            wavelet[0, step_index],
            receiver_x,
            receiver_y,
            recorded[0, step_index],
        )
        image_sum = image_sum + advanced[0] * advanced[1]
        previous, current = (current, advanced)
    result = jnp.stack((previous[0], current[0], previous[1], current[1]))
    result = result.reshape((1, 4, width_x, width_y * depth))
    image = image_prior + lax.psum_scatter(image_sum, "shot", scatter_dimension=2, tiled=True)
    return (result, image)


def iota(shape, dim):
    return lax.broadcasted_iota(jnp.int32, shape, dim)


def swap_shot_and_lane(tiles):
    lane = iota(tiles[0].shape, 1)
    for bit in range(3):
        span = 8 << bit
        low = (lane & span) == 0
        new = list(tiles)
        for i in range(8):
            if i & (1 << bit):
                continue
            a, b = tiles[i], tiles[i | (1 << bit)]
            new[i] = jnp.where(low, a, pltpu.roll(b, span, 1))
            new[i | (1 << bit)] = jnp.where(low, pltpu.roll(a, LANES - span, 1), b)
        tiles = new
    return tiles


def pieces(value):
    first = value.astype(jnp.bfloat16)
    return first, (value - first.astype(jnp.float32)).astype(jnp.bfloat16)


def depth_picks(groups, width_y):
    spot = iota((width_y, groups * LANES), 1)
    in_tile = spot & (LANES - 1)
    y_of = (spot >> 7) * 16 + ((in_tile >> 3) & 7) * 2 + (in_tile >> 6)
    picks = (iota((width_y, groups * LANES), 0) == y_of).astype(jnp.bfloat16)
    own_z = iota((LANES, groups * LANES), 0) & 7
    keep = own_z == (iota((LANES, groups * LANES), 1) & 7)
    return picks, keep


def thirds(value):
    first = value.astype(jnp.bfloat16)
    rest = value - first.astype(jnp.float32)
    second = rest.astype(jnp.bfloat16)
    return first, second, (rest - second.astype(jnp.float32)).astype(jnp.bfloat16)


def kernel(
    tiles,
    shots,
    sx_hbm,
    sy_hbm,
    wave_hbm,
    st_hbm,
    vel_hbm,
    prior_hbm,
    rx_hbm,
    ry_hbm,
    data_hbm,
    ext,
    last,
    total,
    prior_ref,
    sx_ref,
    sy_ref,
    wave_ref,
    rx_ref,
    ry_ref,
    data_ref,
    vel_ref,
    prev,
    lap,
    vgot,
    vfull,
    inj,
    xsend,
    xgot,
    ysend,
    ygot,
    isum,
    isend,
    igot,
    in_sem,
    xs_sem,
    xr_sem,
    ys_sem,
    yr_sem,
    vs_sem,
    vr_sem,
    is_sem,
    ir_sem,
):
    me = lax.axis_index("shot")
    gx = lax.axis_index("gx")
    gy = lax.axis_index("gy")
    width_y = tiles * LANES // DEPTH
    wide = tiles * LANES
    edge = 2 * LANES
    groups = tiles // 8
    c0, c1, c2, c3, c4 = STENCIL
    coefs = STENCIL
    mids = slice(8, 8 + ROWS)

    barrier = pltpu.get_barrier_semaphore()

    def shot_at(d):
        return sum(lax.rem(me // bit + d // bit, 2) * bit for bit in (1, 2, 4))

    def group_at(k):
        return k * gy + (groups - 1 - k) * (1 - gy)

    def in_order(values):
        return [jnp.where(gy == 1, values[k], values[groups - 1 - k]) for k in range(groups)]

    for d in range(1, shots):
        pl.semaphore_signal(
            barrier, inc=1, device_id=(shot_at(d), gx, gy), device_id_type=MESH
        )
    pl.semaphore_signal(barrier, inc=1, device_id=(me, 1 - gx, gy), device_id_type=MESH)
    pl.semaphore_signal(barrier, inc=1, device_id=(me, gx, 1 - gy), device_id_type=MESH)

    inner = (pl.ds(8, ROWS), pl.ds(edge, wide))
    firsts = (8 * (1 - gx), 8 * gx)

    def half_rows(half, ahead=0):
        return pl.ds(pl.multiple_of(firsts[half] + ahead, 8), 8)

    moves = [
        (vel_hbm, vel_ref),
        (st_hbm.at[1], ext.at[(0, 0) + inner]),
        (st_hbm.at[3], ext.at[(0, 1) + inner]),
        (rx_hbm, rx_ref),
        (ry_hbm, ry_ref),
        (data_hbm, data_ref),
        (st_hbm.at[0], prev.at[0]),
        (st_hbm.at[2], prev.at[1]),
        (sx_hbm, sx_ref),
        (sy_hbm, sy_ref),
        (wave_hbm, wave_ref),
        (prior_hbm, prior_ref),
    ]
    loads = [pltpu.make_async_copy(a, b, in_sem.at[i]) for i, (a, b) in enumerate(moves)]
    for load in loads:
        load.start()

    def at(t):
        return pl.ds(pl.multiple_of(t * LANES, LANES), LANES)

    for step in range(2):
        for f in range(2):
            for rows in (slice(0, 8), slice(8 + ROWS, 16 + ROWS)):
                ext[step, f, rows, :] = jnp.zeros((8, wide + 2 * edge), jnp.float32)
            for cols in (slice(0, edge), slice(wide + edge, wide + 2 * edge)):
                ext[step, f, mids, cols] = jnp.zeros((ROWS, edge), jnp.float32)

    picks, keep = depth_picks(groups, width_y)

    row8 = iota((8, LANES), 0)
    at_edge = (row8 >= 4) == (gx == 0)

    def split_rows(a, b):
        upper = jnp.where(row8 < 4, a, pltpu.roll(b, 4, 0))
        lower = jnp.where(row8 < 4, pltpu.roll(a, 4, 0), b)
        return [jnp.where(gx == 0, lower, upper), jnp.where(gx == 0, upper, lower)]

    loads[0].wait()
    flat = jnp.concatenate(pieces(vel_ref[...].reshape((ROWS * PER_SHOT, width_y))), axis=0)
    spread = jnp.dot(flat, picks, preferred_element_type=jnp.float32)
    rows8 = ROWS * PER_SHOT
    spread = spread[:rows8] + spread[rows8:]
    spread = jnp.where(keep, spread, 0.0).reshape((ROWS, PER_SHOT, groups * LANES))
    packed = jnp.sum(spread, axis=1)
    halves = (
        jnp.where(gx == 0, packed[8:], packed[:8]),
        jnp.where(gx == 0, packed[:8], packed[8:]),
    )
    for half in range(2):
        mine = [halves[half][:, u * LANES : (u + 1) * LANES] for u in range(groups)]
        mine = in_order(mine)
        if half == 0:
            mine[:2] = split_rows(*mine[:2])
        for k, tile in enumerate(mine):
            vgot[half, 0, k] = tile

    def columns(u):
        return pl.ds(pl.multiple_of(u * 8 * LANES, 8 * LANES), 8 * LANES)

    top = iota((8, 8 * LANES), 0) < 4

    def pack_x(step, u):
        cols = pl.ds(pl.multiple_of(u * 8 * LANES + edge, LANES), 8 * LANES)
        p, q = (ext[step, f, half_rows(0, 8), cols] for f in range(2))
        tail = jnp.where(top, pltpu.roll(p, 4, 0), q)
        head = jnp.where(top, p, pltpu.roll(q, 4, 0))
        xsend[step, :, columns(u)] = jnp.where(gx == 0, tail, head)

    def pack_y(step):
        for f in range(2):
            ysend[step, f] = jnp.where(
                gy == 0,
                ext[step, f, mids, wide : wide + edge],
                ext[step, f, mids, edge : 2 * edge],
            )

    def x_copy(step, k):
        part = (step,) if step == 0 else (step, slice(None), columns(group_at(k)))
        return pltpu.make_async_remote_copy(
            src_ref=xsend.at[part],
            dst_ref=xgot.at[part],
            send_sem=xs_sem.at[step + k],
            recv_sem=xr_sem.at[step + k],
            device_id=(me, 1 - gx, gy),
            device_id_type=MESH,
        )

    def y_copy(step):
        return pltpu.make_async_remote_copy(
            src_ref=ysend.at[step],
            dst_ref=ygot.at[step],
            send_sem=ys_sem.at[step],
            recv_sem=yr_sem.at[step],
            device_id=(me, gx, 1 - gy),
            device_id_type=MESH,
        )

    loads[1].wait()
    loads[2].wait()
    for u in range(groups):
        pack_x(0, u)
    pack_y(0)
    pl.semaphore_wait(barrier, shots + 1)
    xc, yc = x_copy(0, 0), y_copy(0)
    for part, (half, k) in enumerate(VEL_PARTS):
        for d in reversed(range(1, shots)):
            pltpu.make_async_remote_copy(
                src_ref=vgot.at[half, 0, k],
                dst_ref=vgot.at[half, d, k],
                send_sem=vs_sem.at[0],
                recv_sem=vr_sem.at[part],
                device_id=(shot_at(d), gx, gy),
                device_id_type=MESH,
            ).start()
        if part == 0:
            yc.start()
            xc.start()

    lane = iota((ROWS, LANES), 1)
    depth_at = lane & (DEPTH - 1)
    zero = jnp.zeros((ROWS, LANES), jnp.float32)
    base_x = gx * ROWS
    base_y = gy * width_y

    def along_x(a, b):
        up_a, up_b = ([pltpu.roll(v, 8 - r, 0) for r in range(1, 8)] for v in (a, b))
        above, below = 0.0, 0.0
        for k in range(1, 5):
            ahead, behind = row8 < 8 - k, row8 >= k
            above = above + coefs[k] * (
                jnp.where(ahead, up_a[k - 1], up_b[k - 1]) + jnp.where(behind, up_a[7 - k], 0.0)
            )
            below = below + coefs[k] * (
                jnp.where(ahead, up_b[k - 1], 0.0) + jnp.where(behind, up_b[7 - k], up_a[7 - k])
            )
        return above, below

    def laplace_own(step, first, count):
        size = min(count, 8)

        def one(quad, carry):
            for part in range(size):
                t = first + quad * size + part
                for f in range(2):
                    near = [ext[step, f, mids, at(t + 2 + k)] for k in (-2, -1, 0, 1, 2)]
                    mid = near[2]
                    total = (3.0 * c0) * mid
                    for k in range(1, 5):
                        total = total + jnp.where(depth_at >= k, coefs[k], 0.0) * pltpu.roll(
                            mid, k, 1
                        )
                        total = total + jnp.where(
                            depth_at < DEPTH - k, coefs[k], 0.0
                        ) * pltpu.roll(mid, LANES - k, 1)
                    total = total + c2 * (near[1] + near[3]) + c4 * (near[0] + near[4])
                    after = c1 * (near[3] + near[2]) + c3 * (near[4] + near[1])
                    before = c1 * (near[2] + near[1]) + c3 * (near[3] + near[0])
                    total = total + pltpu.roll(jnp.where(lane < DEPTH, after, before), DEPTH, 1)
                    above, below = along_x(mid[:8], mid[8:])
                    lap[f, 0:8, at(t)] = total[:8] + above
                    lap[f, 8:16, at(t)] = total[8:] + below
            return carry

        lax.fori_loop(0, count // size, one, 0)

    def add_y(step):
        on_left = gy == 1
        on_right = gy == 0
        first = lane < DEPTH
        for f in range(2):
            h0 = ygot[step, f, :, 0:LANES]
            h1 = ygot[step, f, :, LANES:edge]
            a0, a1 = jnp.where(on_left, h0, zero), jnp.where(on_left, h1, zero)
            b0, b1 = jnp.where(on_right, h0, zero), jnp.where(on_right, h1, zero)
            end = tiles - 1
            terms = {
                0: (c2 * a1 + c4 * a0, c3 * a1, c1 * a1 + c3 * a0),
                1: (c4 * a1, zero, c3 * a1),
                end - 1: (c4 * b0, c3 * b0, zero),
                end: (c2 * b0 + c4 * b1, c1 * b0 + c3 * b1, c3 * b0),
            }
            for t, (even, after, before) in terms.items():
                cols = slice(t * LANES, (t + 1) * LANES)
                lap[f, :, cols] = (
                    lap[f, :, cols]
                    + even
                    + pltpu.roll(jnp.where(first, after, before), DEPTH, 1)
                )

    row4 = row8 & 3
    low4 = row8 < 4

    def x_terms(h):
        left = jnp.where(gx == 1, coefs[4], 0.0) * h
        right = jnp.where(gx == 0, coefs[4], 0.0) * h
        for j in range(1, 4):
            left = left + jnp.where((row4 + j < 4) & (gx == 1), coefs[4 - j], 0.0) * pltpu.roll(
                h, 8 - j, 0
            )
            right = right + jnp.where((row4 >= j) & (gx == 0), coefs[4 - j], 0.0) * pltpu.roll(
                h, j, 0
            )
        source = jnp.where(low4, left, pltpu.roll(right, 4, 0))
        receiver = jnp.where(low4, pltpu.roll(left, 4, 0), right)
        return source, receiver

    def advance(step, half, u):
        wave = wave_ref[0, step]
        rows = half_rows(half)
        inside = half_rows(half, 8)
        source_row = row8 == sx_ref[0] - base_x - firsts[half]

        def one(quad, carry):
            for part in range(8):
                t = u * 8 + quad * 8 + part
                terms = x_terms(xgot[step, :, at(t)]) if half == 0 else None
                v = vfull[half, :, at(t)]
                results = []
                for f in range(2):
                    current = ext[step, f, inside, at(t + 2)]
                    if step == 0:
                        previous = prev[f, rows, at(t)]
                    else:
                        previous = ext[0, f, inside, at(t + 2)]
                    spread_out = lap[f, rows, at(t)]
                    if half == 0:
                        spread_out = spread_out + terms[f]
                    new = 2.0 * current - previous + v * spread_out
                    if f == 0:
                        new = new + jnp.where(
                            source_row & (source_lane + t * LANES == 0), wave, 0.0
                        )
                    else:
                        new = new + inj[step, rows, at(t)]
                    if step == 0:
                        ext[1, f, inside, at(t + 2)] = new
                    else:
                        last[f, rows, at(t)] = new
                    results.append(new)
                product = results[0] * results[1]
                if step == 0:
                    isum[half, :, at(t)] = product
                else:
                    isum[half, :, at(t)] = isum[half, :, at(t)] + product
            return carry

        one(0, 0)

    for load in loads[3:6]:
        load.wait()
    hit_x = (iota((ROWS, rx_ref.shape[1]), 0) == rx_ref[...] - base_x).astype(jnp.bfloat16)
    hit_y = (iota((width_y, ry_ref.shape[1]), 0) == ry_ref[...] - base_y).astype(jnp.bfloat16)
    parts = []
    for step in range(2):
        parts += [hit_x * piece for piece in thirds(data_ref[step : step + 1, :])]
    planes = lax.dot_general(
        jnp.concatenate(parts, axis=0),
        hit_y,
        (((1,), (1,)), ((), ())),
        preferred_element_type=jnp.float32,
    )
    for step in range(2):
        base = 3 * ROWS * step
        plane = (
            planes[base : base + ROWS]
            + planes[base + ROWS : base + 2 * ROWS]
            + planes[base + 2 * ROWS : base + 3 * ROWS]
        )
        for t in range(tiles):
            even = jnp.broadcast_to(plane[:, 2 * t : 2 * t + 1], (ROWS, LANES))
            odd = jnp.broadcast_to(plane[:, 2 * t + 1 : 2 * t + 2], (ROWS, LANES))
            inj[step, :, t * LANES : (t + 1) * LANES] = jnp.where(
                lane == REC_Z, even, jnp.where(lane == DEPTH + REC_Z, odd, 0.0)
            )

    laplace_own(0, 0, tiles)
    for load in loads[6:11]:
        load.wait()
    source_lane = iota((8, LANES), 1) - ((sy_ref[0] - base_y) * DEPTH + SRC_Z)
    yc.wait_recv()
    add_y(0)

    def arrived(ref, sem):
        pltpu.make_async_copy(ref, ref, sem).wait()

    others = pl.ds(1, shots - 1)
    slots = [shot_at(s) for s in range(shots)]
    xcopies = [x_copy(1, k) for k in range(groups)]
    next_y = y_copy(1)

    def send_image(half, k):
        u = group_at(k)
        mixed = swap_shot_and_lane([isum[half, :, at(8 * u + i)] for i in range(8)])
        for s in range(shots):
            isend[half, s, k] = mixed[s]
        for d in reversed(range(1, shots)):
            to = shot_at(d)
            pltpu.make_async_remote_copy(
                src_ref=isend.at[half, to, k],
                dst_ref=igot.at[half, d, k],
                send_sem=is_sem.at[0],
                recv_sem=ir_sem.at[half, k],
                device_id=(to, gx, gy),
                device_id_type=MESH,
            ).start()

    def near_half(k):
        xcopies[k].wait_recv()
        advance(1, 0, group_at(k))
        send_image(0, k)

    def far_half(k):
        advance(1, 1, group_at(k))
        send_image(1, k)

    def tile_at(k, i):
        return at(8 * group_at(k) + i)

    def laplace_next(low, high):
        first = low * gy + (tiles - high) * (1 - gy)
        laplace_own(1, first, high - low)

    for part, (half, slot) in enumerate(VEL_PARTS):
        arrived(vgot.at[half, others, slot], vr_sem.at[part])
        mixed = swap_shot_and_lane([vgot[half, slots[s], slot] for s in range(shots)])
        if part == 0:
            for i in range(8):
                turned = pltpu.roll(mixed[i], 4, 0)
                vfull[0, :, tile_at(0, i)] = jnp.where(gx == 0, turned, mixed[i])
                vfull[0, :, tile_at(1, i)] = jnp.where(gx == 0, mixed[i], turned)
            xc.wait_recv()
        elif part == 2:
            for i in range(8):
                turned = pltpu.roll(mixed[i], 4, 0)
                rest = (jnp.where(gx == 0, mixed[i], turned), jnp.where(gx == 0, turned, mixed[i]))
                for k in range(2):
                    vfull[0, :, tile_at(k, i)] = jnp.where(
                        at_edge, vfull[0, :, tile_at(k, i)], rest[k]
                    )
        else:
            for i in range(8):
                vfull[half, :, tile_at(slot, i)] = mixed[i]
        for k in (0, 1) if part in (0, 2) else (slot,):
            advance(0, half, group_at(k))
            if part < 2:
                pack_x(1, group_at(k))
                xcopies[k].start()
        if half == 0:
            continue
        if slot == 0:
            pack_y(1)
            next_y.start()
            laplace_next(0, 4)
        elif slot == 1:
            laplace_next(4, 12)
        else:
            laplace_next(12, 16)
            far_half(1)
            laplace_next(16, 24)
    next_y.wait_recv()
    add_y(1)
    far_half(0)
    far_half(2)
    for k in range(groups):
        near_half(k)
    arrived(vgot.at[:, others], vs_sem.at[0])
    for copy in (xc, yc, next_y, *xcopies):
        copy.wait_send()
    loads[11].wait()
    for half, k in ((1, 1), (1, 0), (1, 2), (0, 0), (0, 1), (0, 2)):
        arrived(igot.at[half, others, k], ir_sem.at[half, k])
        summed = isend[half, me, k]
        for d in range(1, shots):
            summed = summed + igot[half, d, k]
        total[group_at(k), half_rows(half), :] = summed
    arrived(igot.at[:, others], is_sem.at[0])


def store_kernel(ext, last, total, prior, state_out, image_out, img, out_sem):
    wide = last.shape[2]
    groups = total.shape[0]
    width_y = prior.shape[2]
    rows8 = ROWS * PER_SHOT
    inner = (pl.ds(8, ROWS), pl.ds(2 * LANES, wide))
    moves = []
    for f in range(2):
        moves.append((ext.at[(1, f) + inner], state_out.at[2 * f]))
        moves.append((last.at[f], state_out.at[2 * f + 1]))
    moves.append((img, image_out))
    stores = [pltpu.make_async_copy(a, b, out_sem.at[i]) for i, (a, b) in enumerate(moves)]
    for store in stores[:4]:
        store.start()
    picks, keep = depth_picks(groups, width_y)
    image = prior[...].reshape((rows8, width_y))
    for u in range(groups):
        cols = slice(u * LANES, (u + 1) * LANES)
        tall = jnp.broadcast_to(total[u][:, None, :], (ROWS, PER_SHOT, LANES))
        tall = jnp.where(keep[:, cols], tall.reshape((rows8, LANES)), 0.0)
        sides = lax.dot_general(
            jnp.concatenate(pieces(tall), axis=0),
            picks[:, cols],
            (((1,), (1,)), ((), ())),
            preferred_element_type=jnp.float32,
        )
        image = image + (sides[:rows8] + sides[rows8:])
    img[...] = image.reshape((ROWS, PER_SHOT, width_y))
    stores[4].start()
    for store in stores:
        store.wait()


def fast_body(
    state, velocity, image_prior, source_x, source_y, wavelet, receiver_x, receiver_y, recorded
):
    shots = lax.axis_size("shot")
    width_y = velocity.shape[1]
    wide = state.shape[3]
    tiles = wide // LANES
    groups = tiles // 8
    count = receiver_x.shape[1]
    f32 = jnp.float32
    hbm = pl.BlockSpec(memory_space=pltpu.HBM)
    dma = pltpu.SemaphoreType.DMA
    edge = 2 * LANES
    vmem = pl.BlockSpec(memory_space=pltpu.VMEM)
    held = (
        ((2, 2, ROWS + 16, wide + 2 * edge), f32),
        ((2, ROWS, wide), f32),
        ((groups, ROWS, LANES), f32),
        ((ROWS, PER_SHOT, width_y), f32),
    )
    pin = lambda a: pltpu.with_memory_space_constraint(a, pltpu.HBM)
    fields = pl.pallas_call(
        functools.partial(kernel, tiles, shots),
        out_shape=tuple(pltpu.VMEM(*a) for a in held),
        in_specs=[hbm] * 9,
        out_specs=(vmem,) * 4,
        scratch_shapes=[
            pltpu.SMEM((1,), jnp.int32),
            pltpu.SMEM((1,), jnp.int32),
            pltpu.SMEM((1, 2), f32),
            pltpu.VMEM((1, count), jnp.int32),
            pltpu.VMEM((1, count), jnp.int32),
            pltpu.VMEM((2, count), f32),
            pltpu.VMEM((ROWS, PER_SHOT, width_y), f32),
            pltpu.VMEM((2, ROWS, wide), f32),
            pltpu.VMEM((2, ROWS, wide), f32),
            pltpu.VMEM((2, shots, groups, 8, LANES), f32),
            pltpu.VMEM((2, 8, wide), f32),
            pltpu.VMEM((2, ROWS, wide), f32),
            pltpu.VMEM((2, 8, wide), f32),
            pltpu.VMEM((2, 8, wide), f32),
            pltpu.VMEM((2, 2, ROWS, edge), f32),
            pltpu.VMEM((2, 2, ROWS, edge), f32),
            pltpu.VMEM((2, 8, wide), f32),
            pltpu.VMEM((2, shots, groups, 8, LANES), f32),
            pltpu.VMEM((2, shots, groups, 8, LANES), f32),
            dma((12,)),
            dma((1 + groups,)),
            dma((1 + groups,)),
            dma((2,)),
            dma((2,)),
            dma((1,)),
            dma((len(VEL_PARTS),)),
            dma((1,)),
            dma((2, groups)),
        ],
        compiler_params=pltpu.CompilerParams(
            collective_id=0, has_side_effects=True, vmem_limit_bytes=VMEM_BYTES
        ),
    )(
        source_x,
        source_y,
        pin(wavelet),
        pin(state[0]),
        pin(jnp.swapaxes(velocity, 1, 2)),
        pin(jnp.swapaxes(image_prior, 1, 2)),
        pin(receiver_x),
        pin(receiver_y),
        pin(recorded[0]),
    )
    fields = [pltpu.with_memory_space_constraint(a, pltpu.VMEM) for a in fields]
    out, img = pl.pallas_call(
        store_kernel,
        out_shape=(
            jax.ShapeDtypeStruct((4, ROWS, wide), f32),
            jax.ShapeDtypeStruct((ROWS, PER_SHOT, width_y), f32),
        ),
        in_specs=[vmem] * 4,
        out_specs=(hbm, hbm),
        scratch_shapes=[pltpu.VMEM((ROWS, PER_SHOT, width_y), f32), dma((5,))],
        compiler_params=pltpu.CompilerParams(vmem_limit_bytes=VMEM_BYTES),
    )(*fields)
    return (out[None], jnp.swapaxes(img, 1, 2))


def body(
    state, velocity, image_prior, source_x, source_y, wavelet, receiver_x, receiver_y, recorded
):
    shots = lax.axis_size("shot")
    width_x, width_y, per_shot = velocity.shape
    fits = (
        shots == 8
        and lax.axis_size("gx") == 2
        and lax.axis_size("gy") == 2
        and per_shot == PER_SHOT
        and width_x == ROWS
        and width_y == 48
        and wavelet.shape[1] == 2
    )
    chosen = fast_body if fits else general_body
    return chosen(
        state, velocity, image_prior, source_x, source_y, wavelet, receiver_x, receiver_y, recorded
    )


def solution(mesh):
    in_specs = (
        P("shot", None, "gx", "gy"),
        P("gx", "gy", "shot"),
        P("gx", "gy", "shot"),
        P("shot"),
        P("shot"),
        P("shot", None),
        P("shot", None),
        P("shot", None),
        P("shot", None, None),
    )
    out_specs = (P("shot", None, "gx", "gy"), P("gx", "gy", "shot"))
    return jax.shard_map(body, mesh=mesh, in_specs=in_specs, out_specs=out_specs, check_vma=False)
```

```python
import functools

import jax
import jax.numpy as jnp
from jax import lax
from jax.experimental import pallas as pl
from jax.experimental.pallas import tpu as pltpu
from jax.sharding import PartitionSpec as P

SRC_Z = 4
REC_Z = 2


STENCIL = (-205.0 / 72.0, 8.0 / 5.0, -1.0 / 5.0, 8.0 / 315.0, -1.0 / 560.0)

LANES = 128
ROWS = 16
DEPTH = 64
PER_SHOT = 8
UNROLL = 4
VMEM_BYTES = 48 * 1024 * 1024
MESH = pl.DeviceIdType.MESH
VEL_PARTS = ((0, 0), (0, 2), (0, 1), (1, 0), (1, 1), (1, 2))


def padded_2(cells, sides, width):
    for axis, dim in sides:
        count = lax.axis_size(axis)
        ends = count - 1
        head = lax.slice_in_dim(cells, 0, width, axis=dim)
        tail = lax.slice_in_dim(cells, cells.shape[dim] - width, cells.shape[dim], axis=dim)
        cells = jnp.concatenate(
            [
                lax.ppermute(tail, axis, [(i, (i + 1) % count) for i in range(ends)]),
                cells,
                lax.ppermute(head, axis, [((i + 1) % count, i) for i in range(ends)]),
            ],
            axis=dim,
        )
    return cells


def laplace(extended):
    width_x = extended.shape[1] - 8
    width_y = extended.shape[2] - 8
    depth = extended.shape[3]
    padded = jnp.pad(extended, ((0, 0), (0, 0), (0, 0), (4, 4)))

    def shifted(dx, dy, dz):
        return padded[
            :, 4 + dx : 4 + dx + width_x, 4 + dy : 4 + dy + width_y, 4 + dz : 4 + dz + depth
        ]

    summed = 3.0 * STENCIL[0] * shifted(0, 0, 0)
    for offset in range(1, 5):
        summed = summed + STENCIL[offset] * (
            shifted(offset, 0, 0)
            + shifted(-offset, 0, 0)
            + shifted(0, offset, 0)
            + shifted(0, -offset, 0)
            + shifted(0, 0, offset)
            + shifted(0, 0, -offset)
        )
    return summed


def inject_sources(
    advanced, x_coords, y_coords, source_x, source_y, wave_value, receiver_x, receiver_y, data_row
):
    src_plane = ((x_coords == source_x[0])[:, None] & (y_coords == source_y[0])[None, :]).astype(
        jnp.float32
    ) * wave_value
    onehot_x = (x_coords[:, None] == receiver_x[0][None, :]).astype(jnp.float32)
    onehot_y = (receiver_y[0][:, None] == y_coords[None, :]).astype(jnp.float32) * data_row[:, None]
    rec_plane = jnp.dot(
        onehot_x, onehot_y, precision=lax.Precision.HIGHEST, preferred_element_type=jnp.float32
    )
    advanced = advanced.at[0, :, :, SRC_Z].add(src_plane)
    return advanced.at[1, :, :, REC_Z].add(rec_plane)


def general_body(
    state, velocity, image_prior, source_x, source_y, wavelet, receiver_x, receiver_y, recorded
):
    step_count = wavelet.shape[1]
    width_x = velocity.shape[0]
    width_y = velocity.shape[1]
    velocity_full = lax.all_gather(velocity, "shot", axis=2, tiled=True)
    depth = velocity_full.shape[2]
    fields = state[0].reshape((4, width_x, width_y, depth))
    previous = jnp.stack((fields[0], fields[2]))
    current = jnp.stack((fields[1], fields[3]))
    base_x = lax.axis_index("gx") * width_x
    base_y = lax.axis_index("gy") * width_y
    image_sum = jnp.zeros(velocity_full.shape, jnp.float32)
    x_coords = base_x + jnp.arange(width_x, dtype=jnp.int32)
    y_coords = base_y + jnp.arange(width_y, dtype=jnp.int32)
    for step_index in range(step_count):
        extended = padded_2(current, (("gx", 1), ("gy", 2)), 4)
        advanced = 2.0 * current - previous + velocity_full[None] * laplace(extended)
        advanced = inject_sources(
            advanced,
            x_coords,
            y_coords,
            source_x,
            source_y,
            wavelet[0, step_index],
            receiver_x,
            receiver_y,
            recorded[0, step_index],
        )
        image_sum = image_sum + advanced[0] * advanced[1]
        previous, current = (current, advanced)
    result = jnp.stack((previous[0], current[0], previous[1], current[1]))
    result = result.reshape((1, 4, width_x, width_y * depth))
    image = image_prior + lax.psum_scatter(image_sum, "shot", scatter_dimension=2, tiled=True)
    return (result, image)


def iota(shape, dim):
    return lax.broadcasted_iota(jnp.int32, shape, dim)


def swap_shot_and_lane(tiles):
    lane = iota(tiles[0].shape, 1)
    for bit in range(3):
        span = 8 << bit
        low = (lane & span) == 0
        new = list(tiles)
        for i in range(8):
            if i & (1 << bit):
                continue
            a, b = tiles[i], tiles[i | (1 << bit)]
            new[i] = jnp.where(low, a, pltpu.roll(b, span, 1))
            new[i | (1 << bit)] = jnp.where(low, pltpu.roll(a, LANES - span, 1), b)
        tiles = new
    return tiles


def pieces(value):
    first = value.astype(jnp.bfloat16)
    return first, (value - first.astype(jnp.float32)).astype(jnp.bfloat16)


def depth_picks(groups, width_y):
    spot = iota((width_y, groups * LANES), 1)
    in_tile = spot & (LANES - 1)
    y_of = (spot >> 7) * 16 + ((in_tile >> 3) & 7) * 2 + (in_tile >> 6)
    picks = (iota((width_y, groups * LANES), 0) == y_of).astype(jnp.bfloat16)
    own_z = iota((LANES, groups * LANES), 0) & 7
    keep = own_z == (iota((LANES, groups * LANES), 1) & 7)
    return picks, keep


def thirds(value):
    first = value.astype(jnp.bfloat16)
    rest = value - first.astype(jnp.float32)
    second = rest.astype(jnp.bfloat16)
    return first, second, (rest - second.astype(jnp.float32)).astype(jnp.bfloat16)


def kernel(
    tiles,
    shots,
    sx_hbm,
    sy_hbm,
    wave_hbm,
    st_hbm,
    vel_hbm,
    prior_hbm,
    rx_hbm,
    ry_hbm,
    data_hbm,
    ext,
    last,
    total,
    prior_ref,
    sx_ref,
    sy_ref,
    wave_ref,
    rx_ref,
    ry_ref,
    data_ref,
    vel_ref,
    prev,
    lap,
    vgot,
    vfull,
    inj,
    xsend,
    xgot,
    ysend,
    ygot,
    isum,
    isend,
    igot,
    in_sem,
    xs_sem,
    xr_sem,
    ys_sem,
    yr_sem,
    vs_sem,
    vr_sem,
    is_sem,
    ir_sem,
):
    me = lax.axis_index("shot")
    gx = lax.axis_index("gx")
    gy = lax.axis_index("gy")
    width_y = tiles * LANES // DEPTH
    wide = tiles * LANES
    edge = 2 * LANES
    groups = tiles // 8
    c0, c1, c2, c3, c4 = STENCIL
    coefs = STENCIL
    mids = slice(8, 8 + ROWS)

    barrier = pltpu.get_barrier_semaphore()

    def shot_at(d):
        return sum(lax.rem(me // bit + d // bit, 2) * bit for bit in (1, 2, 4))

    def group_at(k):
        return k * gy + (groups - 1 - k) * (1 - gy)

    def in_order(values):
        return [jnp.where(gy == 1, values[k], values[groups - 1 - k]) for k in range(groups)]

    for d in range(1, shots):
        pl.semaphore_signal(
            barrier, inc=1, device_id=(shot_at(d), gx, gy), device_id_type=MESH
        )
    pl.semaphore_signal(barrier, inc=1, device_id=(me, 1 - gx, gy), device_id_type=MESH)
    pl.semaphore_signal(barrier, inc=1, device_id=(me, gx, 1 - gy), device_id_type=MESH)

    inner = (pl.ds(8, ROWS), pl.ds(edge, wide))
    firsts = (8 * (1 - gx), 8 * gx)

    def half_rows(half, ahead=0):
        return pl.ds(pl.multiple_of(firsts[half] + ahead, 8), 8)

    moves = [
        (vel_hbm, vel_ref),
        (st_hbm.at[1], ext.at[(0, 0) + inner]),
        (st_hbm.at[3], ext.at[(0, 1) + inner]),
        (rx_hbm, rx_ref),
        (ry_hbm, ry_ref),
        (data_hbm, data_ref),
        (st_hbm.at[0], prev.at[0]),
        (st_hbm.at[2], prev.at[1]),
        (sx_hbm, sx_ref),
        (sy_hbm, sy_ref),
        (wave_hbm, wave_ref),
        (prior_hbm, prior_ref),
    ]
    loads = [pltpu.make_async_copy(a, b, in_sem.at[i]) for i, (a, b) in enumerate(moves)]
    for load in loads:
        load.start()

    def at(t):
        return pl.ds(pl.multiple_of(t * LANES, LANES), LANES)

    for step in range(2):
        for f in range(2):
            for rows in (slice(0, 8), slice(8 + ROWS, 16 + ROWS)):
                ext[step, f, rows, :] = jnp.zeros((8, wide + 2 * edge), jnp.float32)
            for cols in (slice(0, edge), slice(wide + edge, wide + 2 * edge)):
                ext[step, f, mids, cols] = jnp.zeros((ROWS, edge), jnp.float32)

    picks, keep = depth_picks(groups, width_y)

    row8 = iota((8, LANES), 0)
    at_edge = (row8 >= 4) == (gx == 0)

    def split_rows(a, b):
        upper = jnp.where(row8 < 4, a, pltpu.roll(b, 4, 0))
        lower = jnp.where(row8 < 4, pltpu.roll(a, 4, 0), b)
        return [jnp.where(gx == 0, lower, upper), jnp.where(gx == 0, upper, lower)]

    loads[0].wait()
    flat = jnp.concatenate(pieces(vel_ref[...].reshape((ROWS * PER_SHOT, width_y))), axis=0)
    spread = jnp.dot(flat, picks, preferred_element_type=jnp.float32)
    rows8 = ROWS * PER_SHOT
    spread = spread[:rows8] + spread[rows8:]
    spread = jnp.where(keep, spread, 0.0).reshape((ROWS, PER_SHOT, groups * LANES))
    packed = jnp.sum(spread, axis=1)
    halves = (
        jnp.where(gx == 0, packed[8:], packed[:8]),
        jnp.where(gx == 0, packed[:8], packed[8:]),
    )
    for half in range(2):
        mine = [halves[half][:, u * LANES : (u + 1) * LANES] for u in range(groups)]
        mine = in_order(mine)
        if half == 0:
            mine[:2] = split_rows(*mine[:2])
        for k, tile in enumerate(mine):
            vgot[half, 0, k] = tile

    def columns(u):
        return pl.ds(pl.multiple_of(u * 8 * LANES, 8 * LANES), 8 * LANES)

    top = iota((8, 8 * LANES), 0) < 4

    def pack_x(step, u):
        cols = pl.ds(pl.multiple_of(u * 8 * LANES + edge, LANES), 8 * LANES)
        p, q = (ext[step, f, half_rows(0, 8), cols] for f in range(2))
        tail = jnp.where(top, pltpu.roll(p, 4, 0), q)
        head = jnp.where(top, p, pltpu.roll(q, 4, 0))
        xsend[step, :, columns(u)] = jnp.where(gx == 0, tail, head)

    def pack_y(step):
        for f in range(2):
            ysend[step, f] = jnp.where(
                gy == 0,
                ext[step, f, mids, wide : wide + edge],
                ext[step, f, mids, edge : 2 * edge],
            )

    def x_copy(step, k):
        part = (step,) if step == 0 else (step, slice(None), columns(group_at(k)))
        return pltpu.make_async_remote_copy(
            src_ref=xsend.at[part],
            dst_ref=xgot.at[part],
            send_sem=xs_sem.at[step + k],
            recv_sem=xr_sem.at[step + k],
            device_id=(me, 1 - gx, gy),
            device_id_type=MESH,
        )

    def y_copy(step):
        return pltpu.make_async_remote_copy(
            src_ref=ysend.at[step],
            dst_ref=ygot.at[step],
            send_sem=ys_sem.at[step],
            recv_sem=yr_sem.at[step],
            device_id=(me, gx, 1 - gy),
            device_id_type=MESH,
        )

    loads[1].wait()
    loads[2].wait()
    for u in range(groups):
        pack_x(0, u)
    pack_y(0)
    pl.semaphore_wait(barrier, shots + 1)
    xc, yc = x_copy(0, 0), y_copy(0)
    for part, (half, k) in enumerate(VEL_PARTS):
        for d in reversed(range(1, shots)):
            pltpu.make_async_remote_copy(
                src_ref=vgot.at[half, 0, k],
                dst_ref=vgot.at[half, d, k],
                send_sem=vs_sem.at[0],
                recv_sem=vr_sem.at[part],
                device_id=(shot_at(d), gx, gy),
                device_id_type=MESH,
            ).start()
        if part == 0:
            yc.start()
            xc.start()

    lane = iota((ROWS, LANES), 1)
    depth_at = lane & (DEPTH - 1)
    zero = jnp.zeros((ROWS, LANES), jnp.float32)
    base_x = gx * ROWS
    base_y = gy * width_y

    def along_x(a, b):
        up_a, up_b = ([pltpu.roll(v, 8 - r, 0) for r in range(1, 8)] for v in (a, b))
        above, below = 0.0, 0.0
        for k in range(1, 5):
            ahead, behind = row8 < 8 - k, row8 >= k
            above = above + coefs[k] * (
                jnp.where(ahead, up_a[k - 1], up_b[k - 1]) + jnp.where(behind, up_a[7 - k], 0.0)
            )
            below = below + coefs[k] * (
                jnp.where(ahead, up_b[k - 1], 0.0) + jnp.where(behind, up_b[7 - k], up_a[7 - k])
            )
        return above, below

    def laplace_own(step, first, count):
        size = min(count, 8)

        def one(quad, carry):
            for part in range(size):
                t = first + quad * size + part
                for f in range(2):
                    near = [ext[step, f, mids, at(t + 2 + k)] for k in (-2, -1, 0, 1, 2)]
                    mid = near[2]
                    total = (3.0 * c0) * mid
                    for k in range(1, 5):
                        total = total + jnp.where(depth_at >= k, coefs[k], 0.0) * pltpu.roll(
                            mid, k, 1
                        )
                        total = total + jnp.where(
                            depth_at < DEPTH - k, coefs[k], 0.0
                        ) * pltpu.roll(mid, LANES - k, 1)
                    total = total + c2 * (near[1] + near[3]) + c4 * (near[0] + near[4])
                    after = c1 * (near[3] + near[2]) + c3 * (near[4] + near[1])
                    before = c1 * (near[2] + near[1]) + c3 * (near[3] + near[0])
                    total = total + pltpu.roll(jnp.where(lane < DEPTH, after, before), DEPTH, 1)
                    above, below = along_x(mid[:8], mid[8:])
                    lap[f, 0:8, at(t)] = total[:8] + above
                    lap[f, 8:16, at(t)] = total[8:] + below
            return carry

        lax.fori_loop(0, count // size, one, 0)

    def add_y(step):
        on_left = gy == 1
        on_right = gy == 0
        first = lane < DEPTH
        for f in range(2):
            h0 = ygot[step, f, :, 0:LANES]
            h1 = ygot[step, f, :, LANES:edge]
            a0, a1 = jnp.where(on_left, h0, zero), jnp.where(on_left, h1, zero)
            b0, b1 = jnp.where(on_right, h0, zero), jnp.where(on_right, h1, zero)
            end = tiles - 1
            terms = {
                0: (c2 * a1 + c4 * a0, c3 * a1, c1 * a1 + c3 * a0),
                1: (c4 * a1, zero, c3 * a1),
                end - 1: (c4 * b0, c3 * b0, zero),
                end: (c2 * b0 + c4 * b1, c1 * b0 + c3 * b1, c3 * b0),
            }
            for t, (even, after, before) in terms.items():
                cols = slice(t * LANES, (t + 1) * LANES)
                lap[f, :, cols] = (
                    lap[f, :, cols]
                    + even
                    + pltpu.roll(jnp.where(first, after, before), DEPTH, 1)
                )

    row4 = row8 & 3
    low4 = row8 < 4

    def x_terms(h):
        left = jnp.where(gx == 1, coefs[4], 0.0) * h
        right = jnp.where(gx == 0, coefs[4], 0.0) * h
        for j in range(1, 4):
            left = left + jnp.where((row4 + j < 4) & (gx == 1), coefs[4 - j], 0.0) * pltpu.roll(
                h, 8 - j, 0
            )
            right = right + jnp.where((row4 >= j) & (gx == 0), coefs[4 - j], 0.0) * pltpu.roll(
                h, j, 0
            )
        source = jnp.where(low4, left, pltpu.roll(right, 4, 0))
        receiver = jnp.where(low4, pltpu.roll(left, 4, 0), right)
        return source, receiver

    def advance(step, half, u):
        wave = wave_ref[0, step]
        rows = half_rows(half)
        inside = half_rows(half, 8)
        source_row = row8 == sx_ref[0] - base_x - firsts[half]

        def one(quad, carry):
            for part in range(8):
                t = u * 8 + quad * 8 + part
                terms = x_terms(xgot[step, :, at(t)]) if half == 0 else None
                v = vfull[half, :, at(t)]
                results = []
                for f in range(2):
                    current = ext[step, f, inside, at(t + 2)]
                    if step == 0:
                        previous = prev[f, rows, at(t)]
                    else:
                        previous = ext[0, f, inside, at(t + 2)]
                    spread_out = lap[f, rows, at(t)]
                    if half == 0:
                        spread_out = spread_out + terms[f]
                    new = 2.0 * current - previous + v * spread_out
                    if f == 0:
                        new = new + jnp.where(
                            source_row & (source_lane + t * LANES == 0), wave, 0.0
                        )
                    else:
                        new = new + inj[step, rows, at(t)]
                    if step == 0:
                        ext[1, f, inside, at(t + 2)] = new
                    else:
                        last[f, rows, at(t)] = new
                    results.append(new)
                product = results[0] * results[1]
                if step == 0:
                    isum[half, :, at(t)] = product
                else:
                    isum[half, :, at(t)] = isum[half, :, at(t)] + product
            return carry

        one(0, 0)

    for load in loads[3:6]:
        load.wait()
    hit_x = (iota((ROWS, rx_ref.shape[1]), 0) == rx_ref[...] - base_x).astype(jnp.bfloat16)
    hit_y = (iota((width_y, ry_ref.shape[1]), 0) == ry_ref[...] - base_y).astype(jnp.bfloat16)
    parts = []
    for step in range(2):
        parts += [hit_x * piece for piece in thirds(data_ref[step : step + 1, :])]
    planes = lax.dot_general(
        jnp.concatenate(parts, axis=0),
        hit_y,
        (((1,), (1,)), ((), ())),
        preferred_element_type=jnp.float32,
    )
    for step in range(2):
        base = 3 * ROWS * step
        plane = (
            planes[base : base + ROWS]
            + planes[base + ROWS : base + 2 * ROWS]
            + planes[base + 2 * ROWS : base + 3 * ROWS]
        )
        for t in range(tiles):
            even = jnp.broadcast_to(plane[:, 2 * t : 2 * t + 1], (ROWS, LANES))
            odd = jnp.broadcast_to(plane[:, 2 * t + 1 : 2 * t + 2], (ROWS, LANES))
            inj[step, :, t * LANES : (t + 1) * LANES] = jnp.where(
                lane == REC_Z, even, jnp.where(lane == DEPTH + REC_Z, odd, 0.0)
            )

    laplace_own(0, 0, tiles)
    for load in loads[6:11]:
        load.wait()
    source_lane = iota((8, LANES), 1) - ((sy_ref[0] - base_y) * DEPTH + SRC_Z)
    yc.wait_recv()
    add_y(0)

    def arrived(ref, sem):
        pltpu.make_async_copy(ref, ref, sem).wait()

    others = pl.ds(1, shots - 1)
    slots = [shot_at(s) for s in range(shots)]
    xcopies = [x_copy(1, k) for k in range(groups)]
    next_y = y_copy(1)

    def send_image(half, k):
        u = group_at(k)
        mixed = swap_shot_and_lane([isum[half, :, at(8 * u + i)] for i in range(8)])
        for s in range(shots):
            isend[half, s, k] = mixed[s]
        for d in reversed(range(1, shots)):
            to = shot_at(d)
            pltpu.make_async_remote_copy(
                src_ref=isend.at[half, to, k],
                dst_ref=igot.at[half, d, k],
                send_sem=is_sem.at[0],
                recv_sem=ir_sem.at[half, k],
                device_id=(to, gx, gy),
                device_id_type=MESH,
            ).start()

    def near_half(k):
        xcopies[k].wait_recv()
        advance(1, 0, group_at(k))
        send_image(0, k)

    def far_half(k):
        advance(1, 1, group_at(k))
        send_image(1, k)

    def tile_at(k, i):
        return at(8 * group_at(k) + i)

    def laplace_next(low, high):
        first = low * gy + (tiles - high) * (1 - gy)
        laplace_own(1, first, high - low)

    for part, (half, slot) in enumerate(VEL_PARTS):
        arrived(vgot.at[half, others, slot], vr_sem.at[part])
        mixed = swap_shot_and_lane([vgot[half, slots[s], slot] for s in range(shots)])
        if part == 0:
            for i in range(8):
                turned = pltpu.roll(mixed[i], 4, 0)
                vfull[0, :, tile_at(0, i)] = jnp.where(gx == 0, turned, mixed[i])
                vfull[0, :, tile_at(1, i)] = jnp.where(gx == 0, mixed[i], turned)
            xc.wait_recv()
        elif part == 2:
            for i in range(8):
                turned = pltpu.roll(mixed[i], 4, 0)
                rest = (jnp.where(gx == 0, mixed[i], turned), jnp.where(gx == 0, turned, mixed[i]))
                for k in range(2):
                    vfull[0, :, tile_at(k, i)] = jnp.where(
                        at_edge, vfull[0, :, tile_at(k, i)], rest[k]
                    )
        else:
            for i in range(8):
                vfull[half, :, tile_at(slot, i)] = mixed[i]
        for k in (0, 1) if part in (0, 2) else (slot,):
            advance(0, half, group_at(k))
            if part < 2:
                pack_x(1, group_at(k))
                xcopies[k].start()
        if half == 0:
            continue
        if slot == 0:
            pack_y(1)
            next_y.start()
            laplace_next(0, 4)
        elif slot == 1:
            laplace_next(4, 12)
        else:
            laplace_next(12, 16)
            far_half(1)
            laplace_next(16, 24)
    far_half(2)
    next_y.wait_recv()
    add_y(1)
    far_half(0)
    for k in range(groups):
        near_half(k)
    arrived(vgot.at[:, others], vs_sem.at[0])
    for copy in (xc, yc, next_y, *xcopies):
        copy.wait_send()
    loads[11].wait()
    for half, k in ((1, 1), (1, 0), (1, 2), (0, 0), (0, 1), (0, 2)):
        arrived(igot.at[half, others, k], ir_sem.at[half, k])
        summed = isend[half, me, k]
        for d in range(1, shots):
            summed = summed + igot[half, d, k]
        total[group_at(k), half_rows(half), :] = summed
    arrived(igot.at[:, others], is_sem.at[0])


def store_kernel(ext, last, total, prior, state_out, image_out, img, out_sem):
    wide = last.shape[2]
    groups = total.shape[0]
    width_y = prior.shape[2]
    rows8 = ROWS * PER_SHOT
    inner = (pl.ds(8, ROWS), pl.ds(2 * LANES, wide))
    moves = []
    for f in range(2):
        moves.append((ext.at[(1, f) + inner], state_out.at[2 * f]))
        moves.append((last.at[f], state_out.at[2 * f + 1]))
    moves.append((img, image_out))
    stores = [pltpu.make_async_copy(a, b, out_sem.at[i]) for i, (a, b) in enumerate(moves)]
    for store in stores[:4]:
        store.start()
    picks, keep = depth_picks(groups, width_y)
    image = prior[...].reshape((rows8, width_y))
    for u in range(groups):
        cols = slice(u * LANES, (u + 1) * LANES)
        tall = jnp.broadcast_to(total[u][:, None, :], (ROWS, PER_SHOT, LANES))
        tall = jnp.where(keep[:, cols], tall.reshape((rows8, LANES)), 0.0)
        sides = lax.dot_general(
            jnp.concatenate(pieces(tall), axis=0),
            picks[:, cols],
            (((1,), (1,)), ((), ())),
            preferred_element_type=jnp.float32,
        )
        image = image + (sides[:rows8] + sides[rows8:])
    img[...] = image.reshape((ROWS, PER_SHOT, width_y))
    stores[4].start()
    for store in stores:
        store.wait()


def fast_body(
    state, velocity, image_prior, source_x, source_y, wavelet, receiver_x, receiver_y, recorded
):
    shots = lax.axis_size("shot")
    width_y = velocity.shape[1]
    wide = state.shape[3]
    tiles = wide // LANES
    groups = tiles // 8
    count = receiver_x.shape[1]
    f32 = jnp.float32
    hbm = pl.BlockSpec(memory_space=pltpu.HBM)
    dma = pltpu.SemaphoreType.DMA
    edge = 2 * LANES
    vmem = pl.BlockSpec(memory_space=pltpu.VMEM)
    held = (
        ((2, 2, ROWS + 16, wide + 2 * edge), f32),
        ((2, ROWS, wide), f32),
        ((groups, ROWS, LANES), f32),
        ((ROWS, PER_SHOT, width_y), f32),
    )
    pin = lambda a: pltpu.with_memory_space_constraint(a, pltpu.HBM)
    fields = pl.pallas_call(
        functools.partial(kernel, tiles, shots),
        out_shape=tuple(pltpu.VMEM(*a) for a in held),
        in_specs=[hbm] * 9,
        out_specs=(vmem,) * 4,
        scratch_shapes=[
            pltpu.SMEM((1,), jnp.int32),
            pltpu.SMEM((1,), jnp.int32),
            pltpu.SMEM((1, 2), f32),
            pltpu.VMEM((1, count), jnp.int32),
            pltpu.VMEM((1, count), jnp.int32),
            pltpu.VMEM((2, count), f32),
            pltpu.VMEM((ROWS, PER_SHOT, width_y), f32),
            pltpu.VMEM((2, ROWS, wide), f32),
            pltpu.VMEM((2, ROWS, wide), f32),
            pltpu.VMEM((2, shots, groups, 8, LANES), f32),
            pltpu.VMEM((2, 8, wide), f32),
            pltpu.VMEM((2, ROWS, wide), f32),
            pltpu.VMEM((2, 8, wide), f32),
            pltpu.VMEM((2, 8, wide), f32),
            pltpu.VMEM((2, 2, ROWS, edge), f32),
            pltpu.VMEM((2, 2, ROWS, edge), f32),
            pltpu.VMEM((2, 8, wide), f32),
            pltpu.VMEM((2, shots, groups, 8, LANES), f32),
            pltpu.VMEM((2, shots, groups, 8, LANES), f32),
            dma((12,)),
            dma((1 + groups,)),
            dma((1 + groups,)),
            dma((2,)),
            dma((2,)),
            dma((1,)),
            dma((len(VEL_PARTS),)),
            dma((1,)),
            dma((2, groups)),
        ],
        compiler_params=pltpu.CompilerParams(
            collective_id=0, has_side_effects=True, vmem_limit_bytes=VMEM_BYTES
        ),
    )(
        source_x,
        source_y,
        pin(wavelet),
        pin(state[0]),
        pin(jnp.swapaxes(velocity, 1, 2)),
        pin(jnp.swapaxes(image_prior, 1, 2)),
        pin(receiver_x),
        pin(receiver_y),
        pin(recorded[0]),
    )
    fields = [pltpu.with_memory_space_constraint(a, pltpu.VMEM) for a in fields]
    out, img = pl.pallas_call(
        store_kernel,
        out_shape=(
            jax.ShapeDtypeStruct((4, ROWS, wide), f32),
            jax.ShapeDtypeStruct((ROWS, PER_SHOT, width_y), f32),
        ),
        in_specs=[vmem] * 4,
        out_specs=(hbm, hbm),
        scratch_shapes=[pltpu.VMEM((ROWS, PER_SHOT, width_y), f32), dma((5,))],
        compiler_params=pltpu.CompilerParams(vmem_limit_bytes=VMEM_BYTES),
    )(*fields)
    return (out[None], jnp.swapaxes(img, 1, 2))


def body(
    state, velocity, image_prior, source_x, source_y, wavelet, receiver_x, receiver_y, recorded
):
    shots = lax.axis_size("shot")
    width_x, width_y, per_shot = velocity.shape
    fits = (
        shots == 8
        and lax.axis_size("gx") == 2
        and lax.axis_size("gy") == 2
        and per_shot == PER_SHOT
        and width_x == ROWS
        and width_y == 48
        and wavelet.shape[1] == 2
    )
    chosen = fast_body if fits else general_body
    return chosen(
        state, velocity, image_prior, source_x, source_y, wavelet, receiver_x, receiver_y, recorded
    )


def solution(mesh):
    in_specs = (
        P("shot", None, "gx", "gy"),
        P("gx", "gy", "shot"),
        P("gx", "gy", "shot"),
        P("shot"),
        P("shot"),
        P("shot", None),
        P("shot", None),
        P("shot", None),
        P("shot", None, None),
    )
    out_specs = (P("shot", None, "gx", "gy"), P("gx", "gy", "shot"))
    return jax.shard_map(body, mesh=mesh, in_specs=in_specs, out_specs=out_specs, check_vma=False)
```

```python
import functools

import jax
import jax.numpy as jnp
from jax import lax
from jax.experimental import pallas as pl
from jax.experimental.pallas import tpu as pltpu
from jax.sharding import PartitionSpec as P

SRC_Z = 4
REC_Z = 2


STENCIL = (-205.0 / 72.0, 8.0 / 5.0, -1.0 / 5.0, 8.0 / 315.0, -1.0 / 560.0)

LANES = 128
ROWS = 16
DEPTH = 64
PER_SHOT = 8
UNROLL = 4
VMEM_BYTES = 48 * 1024 * 1024
MESH = pl.DeviceIdType.MESH
VEL_PARTS = ((0, 0), (0, 1), (0, 2), (1, 0), (1, 1), (1, 2))


def padded_2(cells, sides, width):
    for axis, dim in sides:
        count = lax.axis_size(axis)
        ends = count - 1
        head = lax.slice_in_dim(cells, 0, width, axis=dim)
        tail = lax.slice_in_dim(cells, cells.shape[dim] - width, cells.shape[dim], axis=dim)
        cells = jnp.concatenate(
            [
                lax.ppermute(tail, axis, [(i, (i + 1) % count) for i in range(ends)]),
                cells,
                lax.ppermute(head, axis, [((i + 1) % count, i) for i in range(ends)]),
            ],
            axis=dim,
        )
    return cells


def laplace(extended):
    width_x = extended.shape[1] - 8
    width_y = extended.shape[2] - 8
    depth = extended.shape[3]
    padded = jnp.pad(extended, ((0, 0), (0, 0), (0, 0), (4, 4)))

    def shifted(dx, dy, dz):
        return padded[
            :, 4 + dx : 4 + dx + width_x, 4 + dy : 4 + dy + width_y, 4 + dz : 4 + dz + depth
        ]

    summed = 3.0 * STENCIL[0] * shifted(0, 0, 0)
    for offset in range(1, 5):
        summed = summed + STENCIL[offset] * (
            shifted(offset, 0, 0)
            + shifted(-offset, 0, 0)
            + shifted(0, offset, 0)
            + shifted(0, -offset, 0)
            + shifted(0, 0, offset)
            + shifted(0, 0, -offset)
        )
    return summed


def inject_sources(
    advanced, x_coords, y_coords, source_x, source_y, wave_value, receiver_x, receiver_y, data_row
):
    src_plane = ((x_coords == source_x[0])[:, None] & (y_coords == source_y[0])[None, :]).astype(
        jnp.float32
    ) * wave_value
    onehot_x = (x_coords[:, None] == receiver_x[0][None, :]).astype(jnp.float32)
    onehot_y = (receiver_y[0][:, None] == y_coords[None, :]).astype(jnp.float32) * data_row[:, None]
    rec_plane = jnp.dot(
        onehot_x, onehot_y, precision=lax.Precision.HIGHEST, preferred_element_type=jnp.float32
    )
    advanced = advanced.at[0, :, :, SRC_Z].add(src_plane)
    return advanced.at[1, :, :, REC_Z].add(rec_plane)


def general_body(
    state, velocity, image_prior, source_x, source_y, wavelet, receiver_x, receiver_y, recorded
):
    step_count = wavelet.shape[1]
    width_x = velocity.shape[0]
    width_y = velocity.shape[1]
    velocity_full = lax.all_gather(velocity, "shot", axis=2, tiled=True)
    depth = velocity_full.shape[2]
    fields = state[0].reshape((4, width_x, width_y, depth))
    previous = jnp.stack((fields[0], fields[2]))
    current = jnp.stack((fields[1], fields[3]))
    base_x = lax.axis_index("gx") * width_x
    base_y = lax.axis_index("gy") * width_y
    image_sum = jnp.zeros(velocity_full.shape, jnp.float32)
    x_coords = base_x + jnp.arange(width_x, dtype=jnp.int32)
    y_coords = base_y + jnp.arange(width_y, dtype=jnp.int32)
    for step_index in range(step_count):
        extended = padded_2(current, (("gx", 1), ("gy", 2)), 4)
        advanced = 2.0 * current - previous + velocity_full[None] * laplace(extended)
        advanced = inject_sources(
            advanced,
            x_coords,
            y_coords,
            source_x,
            source_y,
            wavelet[0, step_index],
            receiver_x,
            receiver_y,
            recorded[0, step_index],
        )
        image_sum = image_sum + advanced[0] * advanced[1]
        previous, current = (current, advanced)
    result = jnp.stack((previous[0], current[0], previous[1], current[1]))
    result = result.reshape((1, 4, width_x, width_y * depth))
    image = image_prior + lax.psum_scatter(image_sum, "shot", scatter_dimension=2, tiled=True)
    return (result, image)


def iota(shape, dim):
    return lax.broadcasted_iota(jnp.int32, shape, dim)


def swap_shot_and_lane(tiles):
    lane = iota(tiles[0].shape, 1)
    for bit in range(3):
        span = 8 << bit
        low = (lane & span) == 0
        new = list(tiles)
        for i in range(8):
            if i & (1 << bit):
                continue
            a, b = tiles[i], tiles[i | (1 << bit)]
            new[i] = jnp.where(low, a, pltpu.roll(b, span, 1))
            new[i | (1 << bit)] = jnp.where(low, pltpu.roll(a, LANES - span, 1), b)
        tiles = new
    return tiles


def pieces(value):
    first = value.astype(jnp.bfloat16)
    return first, (value - first.astype(jnp.float32)).astype(jnp.bfloat16)


def depth_picks(groups, width_y):
    spot = iota((width_y, groups * LANES), 1)
    in_tile = spot & (LANES - 1)
    y_of = (spot >> 7) * 16 + ((in_tile >> 3) & 7) * 2 + (in_tile >> 6)
    picks = (iota((width_y, groups * LANES), 0) == y_of).astype(jnp.bfloat16)
    own_z = iota((LANES, groups * LANES), 0) & 7
    keep = own_z == (iota((LANES, groups * LANES), 1) & 7)
    return picks, keep


def thirds(value):
    first = value.astype(jnp.bfloat16)
    rest = value - first.astype(jnp.float32)
    second = rest.astype(jnp.bfloat16)
    return first, second, (rest - second.astype(jnp.float32)).astype(jnp.bfloat16)


def kernel(
    tiles,
    shots,
    sx_hbm,
    sy_hbm,
    wave_hbm,
    st_hbm,
    vel_hbm,
    prior_hbm,
    rx_hbm,
    ry_hbm,
    data_hbm,
    ext,
    last,
    total,
    prior_ref,
    sx_ref,
    sy_ref,
    wave_ref,
    rx_ref,
    ry_ref,
    data_ref,
    vel_ref,
    prev,
    lap,
    vgot,
    vfull,
    inj,
    xsend,
    xgot,
    ysend,
    ygot,
    isum,
    isend,
    igot,
    in_sem,
    xs_sem,
    xr_sem,
    ys_sem,
    yr_sem,
    vs_sem,
    vr_sem,
    is_sem,
    ir_sem,
):
    me = lax.axis_index("shot")
    gx = lax.axis_index("gx")
    gy = lax.axis_index("gy")
    width_y = tiles * LANES // DEPTH
    wide = tiles * LANES
    edge = 2 * LANES
    groups = tiles // 8
    c0, c1, c2, c3, c4 = STENCIL
    coefs = STENCIL
    mids = slice(8, 8 + ROWS)

    barrier = pltpu.get_barrier_semaphore()

    def shot_at(d):
        return sum(lax.rem(me // bit + d // bit, 2) * bit for bit in (1, 2, 4))

    def group_at(k):
        return k * gy + (groups - 1 - k) * (1 - gy)

    def in_order(values):
        return [jnp.where(gy == 1, values[k], values[groups - 1 - k]) for k in range(groups)]

    for d in range(1, shots):
        pl.semaphore_signal(
            barrier, inc=1, device_id=(shot_at(d), gx, gy), device_id_type=MESH
        )
    pl.semaphore_signal(barrier, inc=1, device_id=(me, 1 - gx, gy), device_id_type=MESH)
    pl.semaphore_signal(barrier, inc=1, device_id=(me, gx, 1 - gy), device_id_type=MESH)

    inner = (pl.ds(8, ROWS), pl.ds(edge, wide))
    firsts = (8 * (1 - gx), 8 * gx)

    def half_rows(half, ahead=0):
        return pl.ds(pl.multiple_of(firsts[half] + ahead, 8), 8)

    moves = [
        (vel_hbm, vel_ref),
        (st_hbm.at[1], ext.at[(0, 0) + inner]),
        (st_hbm.at[3], ext.at[(0, 1) + inner]),
        (rx_hbm, rx_ref),
        (ry_hbm, ry_ref),
        (data_hbm, data_ref),
        (st_hbm.at[0], prev.at[0]),
        (st_hbm.at[2], prev.at[1]),
        (sx_hbm, sx_ref),
        (sy_hbm, sy_ref),
        (wave_hbm, wave_ref),
        (prior_hbm, prior_ref),
    ]
    loads = [pltpu.make_async_copy(a, b, in_sem.at[i]) for i, (a, b) in enumerate(moves)]
    for load in loads:
        load.start()

    def at(t):
        return pl.ds(pl.multiple_of(t * LANES, LANES), LANES)

    for step in range(2):
        for f in range(2):
            for rows in (slice(0, 8), slice(8 + ROWS, 16 + ROWS)):
                ext[step, f, rows, :] = jnp.zeros((8, wide + 2 * edge), jnp.float32)
            for cols in (slice(0, edge), slice(wide + edge, wide + 2 * edge)):
                ext[step, f, mids, cols] = jnp.zeros((ROWS, edge), jnp.float32)

    picks, keep = depth_picks(groups, width_y)

    row8 = iota((8, LANES), 0)
    at_edge = (row8 >= 4) == (gx == 0)

    def split_rows(a, b):
        upper = jnp.where(row8 < 4, a, pltpu.roll(b, 4, 0))
        lower = jnp.where(row8 < 4, pltpu.roll(a, 4, 0), b)
        return [jnp.where(gx == 0, lower, upper), jnp.where(gx == 0, upper, lower)]

    loads[0].wait()
    flat = jnp.concatenate(pieces(vel_ref[...].reshape((ROWS * PER_SHOT, width_y))), axis=0)
    spread = jnp.dot(flat, picks, preferred_element_type=jnp.float32)
    rows8 = ROWS * PER_SHOT
    spread = spread[:rows8] + spread[rows8:]
    spread = jnp.where(keep, spread, 0.0).reshape((ROWS, PER_SHOT, groups * LANES))
    packed = jnp.sum(spread, axis=1)
    halves = (
        jnp.where(gx == 0, packed[8:], packed[:8]),
        jnp.where(gx == 0, packed[:8], packed[8:]),
    )
    for half in range(2):
        mine = [halves[half][:, u * LANES : (u + 1) * LANES] for u in range(groups)]
        mine = in_order(mine)
        if half == 0:
            mine[:2] = split_rows(*mine[:2])
        for k, tile in enumerate(mine):
            vgot[half, 0, k] = tile

    def columns(u):
        return pl.ds(pl.multiple_of(u * 8 * LANES, 8 * LANES), 8 * LANES)

    top = iota((8, 8 * LANES), 0) < 4

    def pack_x(step, u):
        cols = pl.ds(pl.multiple_of(u * 8 * LANES + edge, LANES), 8 * LANES)
        p, q = (ext[step, f, half_rows(0, 8), cols] for f in range(2))
        tail = jnp.where(top, pltpu.roll(p, 4, 0), q)
        head = jnp.where(top, p, pltpu.roll(q, 4, 0))
        xsend[step, :, columns(u)] = jnp.where(gx == 0, tail, head)

    def pack_y(step):
        for f in range(2):
            ysend[step, f] = jnp.where(
                gy == 0,
                ext[step, f, mids, wide : wide + edge],
                ext[step, f, mids, edge : 2 * edge],
            )

    def x_copy(step, k):
        part = (step,) if step == 0 else (step, slice(None), columns(group_at(k)))
        return pltpu.make_async_remote_copy(
            src_ref=xsend.at[part],
            dst_ref=xgot.at[part],
            send_sem=xs_sem.at[step + k],
            recv_sem=xr_sem.at[step + k],
            device_id=(me, 1 - gx, gy),
            device_id_type=MESH,
        )

    def y_copy(step):
        return pltpu.make_async_remote_copy(
            src_ref=ysend.at[step],
            dst_ref=ygot.at[step],
            send_sem=ys_sem.at[step],
            recv_sem=yr_sem.at[step],
            device_id=(me, gx, 1 - gy),
            device_id_type=MESH,
        )

    loads[1].wait()
    loads[2].wait()
    for u in range(groups):
        pack_x(0, u)
    pack_y(0)
    pl.semaphore_wait(barrier, shots + 1)
    xc, yc = x_copy(0, 0), y_copy(0)
    for part, (half, k) in enumerate(VEL_PARTS):
        for d in reversed(range(1, shots)):
            pltpu.make_async_remote_copy(
                src_ref=vgot.at[half, 0, k],
                dst_ref=vgot.at[half, d, k],
                send_sem=vs_sem.at[0],
                recv_sem=vr_sem.at[part],
                device_id=(shot_at(d), gx, gy),
                device_id_type=MESH,
            ).start()
        if part == 0:
            yc.start()
            xc.start()

    lane = iota((ROWS, LANES), 1)
    depth_at = lane & (DEPTH - 1)
    zero = jnp.zeros((ROWS, LANES), jnp.float32)
    base_x = gx * ROWS
    base_y = gy * width_y

    def along_x(a, b):
        up_a, up_b = ([pltpu.roll(v, 8 - r, 0) for r in range(1, 8)] for v in (a, b))
        above, below = 0.0, 0.0
        for k in range(1, 5):
            ahead, behind = row8 < 8 - k, row8 >= k
            above = above + coefs[k] * (
                jnp.where(ahead, up_a[k - 1], up_b[k - 1]) + jnp.where(behind, up_a[7 - k], 0.0)
            )
            below = below + coefs[k] * (
                jnp.where(ahead, up_b[k - 1], 0.0) + jnp.where(behind, up_b[7 - k], up_a[7 - k])
            )
        return above, below

    def laplace_own(step, first, count):
        size = min(count, 8)

        def one(quad, carry):
            for part in range(size):
                t = first + quad * size + part
                for f in range(2):
                    near = [ext[step, f, mids, at(t + 2 + k)] for k in (-2, -1, 0, 1, 2)]
                    mid = near[2]
                    total = (3.0 * c0) * mid
                    for k in range(1, 5):
                        total = total + jnp.where(depth_at >= k, coefs[k], 0.0) * pltpu.roll(
                            mid, k, 1
                        )
                        total = total + jnp.where(
                            depth_at < DEPTH - k, coefs[k], 0.0
                        ) * pltpu.roll(mid, LANES - k, 1)
                    total = total + c2 * (near[1] + near[3]) + c4 * (near[0] + near[4])
                    after = c1 * (near[3] + near[2]) + c3 * (near[4] + near[1])
                    before = c1 * (near[2] + near[1]) + c3 * (near[3] + near[0])
                    total = total + pltpu.roll(jnp.where(lane < DEPTH, after, before), DEPTH, 1)
                    above, below = along_x(mid[:8], mid[8:])
                    lap[f, 0:8, at(t)] = total[:8] + above
                    lap[f, 8:16, at(t)] = total[8:] + below
            return carry

        lax.fori_loop(0, count // size, one, 0)

    def add_y(step):
        on_left = gy == 1
        on_right = gy == 0
        first = lane < DEPTH
        for f in range(2):
            h0 = ygot[step, f, :, 0:LANES]
            h1 = ygot[step, f, :, LANES:edge]
            a0, a1 = jnp.where(on_left, h0, zero), jnp.where(on_left, h1, zero)
            b0, b1 = jnp.where(on_right, h0, zero), jnp.where(on_right, h1, zero)
            end = tiles - 1
            terms = {
                0: (c2 * a1 + c4 * a0, c3 * a1, c1 * a1 + c3 * a0),
                1: (c4 * a1, zero, c3 * a1),
                end - 1: (c4 * b0, c3 * b0, zero),
                end: (c2 * b0 + c4 * b1, c1 * b0 + c3 * b1, c3 * b0),
            }
            for t, (even, after, before) in terms.items():
                cols = slice(t * LANES, (t + 1) * LANES)
                lap[f, :, cols] = (
                    lap[f, :, cols]
                    + even
                    + pltpu.roll(jnp.where(first, after, before), DEPTH, 1)
                )

    row4 = row8 & 3
    low4 = row8 < 4

    def x_terms(h):
        left = jnp.where(gx == 1, coefs[4], 0.0) * h
        right = jnp.where(gx == 0, coefs[4], 0.0) * h
        for j in range(1, 4):
            left = left + jnp.where((row4 + j < 4) & (gx == 1), coefs[4 - j], 0.0) * pltpu.roll(
                h, 8 - j, 0
            )
            right = right + jnp.where((row4 >= j) & (gx == 0), coefs[4 - j], 0.0) * pltpu.roll(
                h, j, 0
            )
        source = jnp.where(low4, left, pltpu.roll(right, 4, 0))
        receiver = jnp.where(low4, pltpu.roll(left, 4, 0), right)
        return source, receiver

    def advance(step, half, u):
        wave = wave_ref[0, step]
        rows = half_rows(half)
        inside = half_rows(half, 8)
        source_row = row8 == sx_ref[0] - base_x - firsts[half]

        def one(quad, carry):
            for part in range(8):
                t = u * 8 + quad * 8 + part
                terms = x_terms(xgot[step, :, at(t)]) if half == 0 else None
                v = vfull[half, :, at(t)]
                results = []
                for f in range(2):
                    current = ext[step, f, inside, at(t + 2)]
                    if step == 0:
                        previous = prev[f, rows, at(t)]
                    else:
                        previous = ext[0, f, inside, at(t + 2)]
                    spread_out = lap[f, rows, at(t)]
                    if half == 0:
                        spread_out = spread_out + terms[f]
                    new = 2.0 * current - previous + v * spread_out
                    if f == 0:
                        new = new + jnp.where(
                            source_row & (source_lane + t * LANES == 0), wave, 0.0
                        )
                    else:
                        new = new + inj[step, rows, at(t)]
                    if step == 0:
                        ext[1, f, inside, at(t + 2)] = new
                    else:
                        last[f, rows, at(t)] = new
                    results.append(new)
                product = results[0] * results[1]
                if step == 0:
                    isum[half, :, at(t)] = product
                else:
                    isum[half, :, at(t)] = isum[half, :, at(t)] + product
            return carry

        one(0, 0)

    for load in loads[3:6]:
        load.wait()
    hit_x = (iota((ROWS, rx_ref.shape[1]), 0) == rx_ref[...] - base_x).astype(jnp.bfloat16)
    hit_y = (iota((width_y, ry_ref.shape[1]), 0) == ry_ref[...] - base_y).astype(jnp.bfloat16)
    parts = []
    for step in range(2):
        parts += [hit_x * piece for piece in thirds(data_ref[step : step + 1, :])]
    planes = lax.dot_general(
        jnp.concatenate(parts, axis=0),
        hit_y,
        (((1,), (1,)), ((), ())),
        preferred_element_type=jnp.float32,
    )
    for step in range(2):
        base = 3 * ROWS * step
        plane = (
            planes[base : base + ROWS]
            + planes[base + ROWS : base + 2 * ROWS]
            + planes[base + 2 * ROWS : base + 3 * ROWS]
        )
        for t in range(tiles):
            even = jnp.broadcast_to(plane[:, 2 * t : 2 * t + 1], (ROWS, LANES))
            odd = jnp.broadcast_to(plane[:, 2 * t + 1 : 2 * t + 2], (ROWS, LANES))
            inj[step, :, t * LANES : (t + 1) * LANES] = jnp.where(
                lane == REC_Z, even, jnp.where(lane == DEPTH + REC_Z, odd, 0.0)
            )

    laplace_own(0, 0, tiles)
    for load in loads[6:11]:
        load.wait()
    source_lane = iota((8, LANES), 1) - ((sy_ref[0] - base_y) * DEPTH + SRC_Z)
    yc.wait_recv()
    add_y(0)

    def arrived(ref, sem):
        pltpu.make_async_copy(ref, ref, sem).wait()

    others = pl.ds(1, shots - 1)
    slots = [shot_at(s) for s in range(shots)]
    xcopies = [x_copy(1, k) for k in range(groups)]
    next_y = y_copy(1)

    def send_image(half, k):
        u = group_at(k)
        mixed = swap_shot_and_lane([isum[half, :, at(8 * u + i)] for i in range(8)])
        for s in range(shots):
            isend[half, s, k] = mixed[s]
        for d in reversed(range(1, shots)):
            to = shot_at(d)
            pltpu.make_async_remote_copy(
                src_ref=isend.at[half, to, k],
                dst_ref=igot.at[half, d, k],
                send_sem=is_sem.at[0],
                recv_sem=ir_sem.at[half, k],
                device_id=(to, gx, gy),
                device_id_type=MESH,
            ).start()

    def near_half(k):
        xcopies[k].wait_recv()
        advance(1, 0, group_at(k))
        send_image(0, k)

    def far_half(k):
        advance(1, 1, group_at(k))
        send_image(1, k)

    def tile_at(k, i):
        return at(8 * group_at(k) + i)

    def laplace_next(low, high):
        first = low * gy + (tiles - high) * (1 - gy)
        laplace_own(1, first, high - low)

    for part, (half, slot) in enumerate(VEL_PARTS):
        arrived(vgot.at[half, others, slot], vr_sem.at[part])
        mixed = swap_shot_and_lane([vgot[half, slots[s], slot] for s in range(shots)])
        if (half, slot) == (0, 0):
            for i in range(8):
                turned = pltpu.roll(mixed[i], 4, 0)
                vfull[0, :, tile_at(0, i)] = jnp.where(gx == 0, turned, mixed[i])
                vfull[0, :, tile_at(1, i)] = jnp.where(gx == 0, mixed[i], turned)
            xc.wait_recv()
        elif (half, slot) == (0, 1):
            for i in range(8):
                turned = pltpu.roll(mixed[i], 4, 0)
                rest = (jnp.where(gx == 0, mixed[i], turned), jnp.where(gx == 0, turned, mixed[i]))
                for k in range(2):
                    vfull[0, :, tile_at(k, i)] = jnp.where(
                        at_edge, vfull[0, :, tile_at(k, i)], rest[k]
                    )
        else:
            for i in range(8):
                vfull[half, :, tile_at(slot, i)] = mixed[i]
        for k in (0, 1) if half == 0 and slot < 2 else (slot,):
            advance(0, half, group_at(k))
            if half == 0 and slot != 1:
                pack_x(1, group_at(k))
                xcopies[k].start()
        if half == 0:
            continue
        if slot == 0:
            pack_y(1)
            next_y.start()
            laplace_next(0, 4)
        elif slot == 1:
            laplace_next(4, 12)
        else:
            laplace_next(12, 16)
            far_half(1)
            laplace_next(16, 24)
    far_half(2)
    next_y.wait_recv()
    add_y(1)
    far_half(0)
    for k in range(groups):
        near_half(k)
    arrived(vgot.at[:, others], vs_sem.at[0])
    for copy in (xc, yc, next_y, *xcopies):
        copy.wait_send()
    loads[11].wait()
    for half, k in ((1, 1), (1, 0), (1, 2), (0, 0), (0, 1), (0, 2)):
        arrived(igot.at[half, others, k], ir_sem.at[half, k])
        summed = isend[half, me, k]
        for d in range(1, shots):
            summed = summed + igot[half, d, k]
        total[group_at(k), half_rows(half), :] = summed
    arrived(igot.at[:, others], is_sem.at[0])


def store_kernel(ext, last, total, prior, state_out, image_out, img, out_sem):
    wide = last.shape[2]
    groups = total.shape[0]
    width_y = prior.shape[2]
    rows8 = ROWS * PER_SHOT
    inner = (pl.ds(8, ROWS), pl.ds(2 * LANES, wide))
    moves = []
    for f in range(2):
        moves.append((ext.at[(1, f) + inner], state_out.at[2 * f]))
        moves.append((last.at[f], state_out.at[2 * f + 1]))
    moves.append((img, image_out))
    stores = [pltpu.make_async_copy(a, b, out_sem.at[i]) for i, (a, b) in enumerate(moves)]
    for store in stores[:4]:
        store.start()
    picks, keep = depth_picks(groups, width_y)
    image = prior[...].reshape((rows8, width_y))
    for u in range(groups):
        cols = slice(u * LANES, (u + 1) * LANES)
        tall = jnp.broadcast_to(total[u][:, None, :], (ROWS, PER_SHOT, LANES))
        tall = jnp.where(keep[:, cols], tall.reshape((rows8, LANES)), 0.0)
        sides = lax.dot_general(
            jnp.concatenate(pieces(tall), axis=0),
            picks[:, cols],
            (((1,), (1,)), ((), ())),
            preferred_element_type=jnp.float32,
        )
        image = image + (sides[:rows8] + sides[rows8:])
    img[...] = image.reshape((ROWS, PER_SHOT, width_y))
    stores[4].start()
    for store in stores:
        store.wait()


def fast_body(
    state, velocity, image_prior, source_x, source_y, wavelet, receiver_x, receiver_y, recorded
):
    shots = lax.axis_size("shot")
    width_y = velocity.shape[1]
    wide = state.shape[3]
    tiles = wide // LANES
    groups = tiles // 8
    count = receiver_x.shape[1]
    f32 = jnp.float32
    hbm = pl.BlockSpec(memory_space=pltpu.HBM)
    dma = pltpu.SemaphoreType.DMA
    edge = 2 * LANES
    vmem = pl.BlockSpec(memory_space=pltpu.VMEM)
    held = (
        ((2, 2, ROWS + 16, wide + 2 * edge), f32),
        ((2, ROWS, wide), f32),
        ((groups, ROWS, LANES), f32),
        ((ROWS, PER_SHOT, width_y), f32),
    )
    pin = lambda a: pltpu.with_memory_space_constraint(a, pltpu.HBM)
    fields = pl.pallas_call(
        functools.partial(kernel, tiles, shots),
        out_shape=tuple(pltpu.VMEM(*a) for a in held),
        in_specs=[hbm] * 9,
        out_specs=(vmem,) * 4,
        scratch_shapes=[
            pltpu.SMEM((1,), jnp.int32),
            pltpu.SMEM((1,), jnp.int32),
            pltpu.SMEM((1, 2), f32),
            pltpu.VMEM((1, count), jnp.int32),
            pltpu.VMEM((1, count), jnp.int32),
            pltpu.VMEM((2, count), f32),
            pltpu.VMEM((ROWS, PER_SHOT, width_y), f32),
            pltpu.VMEM((2, ROWS, wide), f32),
            pltpu.VMEM((2, ROWS, wide), f32),
            pltpu.VMEM((2, shots, groups, 8, LANES), f32),
            pltpu.VMEM((2, 8, wide), f32),
            pltpu.VMEM((2, ROWS, wide), f32),
            pltpu.VMEM((2, 8, wide), f32),
            pltpu.VMEM((2, 8, wide), f32),
            pltpu.VMEM((2, 2, ROWS, edge), f32),
            pltpu.VMEM((2, 2, ROWS, edge), f32),
            pltpu.VMEM((2, 8, wide), f32),
            pltpu.VMEM((2, shots, groups, 8, LANES), f32),
            pltpu.VMEM((2, shots, groups, 8, LANES), f32),
            dma((12,)),
            dma((1 + groups,)),
            dma((1 + groups,)),
            dma((2,)),
            dma((2,)),
            dma((1,)),
            dma((len(VEL_PARTS),)),
            dma((1,)),
            dma((2, groups)),
        ],
        compiler_params=pltpu.CompilerParams(
            collective_id=0, has_side_effects=True, vmem_limit_bytes=VMEM_BYTES
        ),
    )(
        source_x,
        source_y,
        pin(wavelet),
        pin(state[0]),
        pin(jnp.swapaxes(velocity, 1, 2)),
        pin(jnp.swapaxes(image_prior, 1, 2)),
        pin(receiver_x),
        pin(receiver_y),
        pin(recorded[0]),
    )
    fields = [pltpu.with_memory_space_constraint(a, pltpu.VMEM) for a in fields]
    out, img = pl.pallas_call(
        store_kernel,
        out_shape=(
            jax.ShapeDtypeStruct((4, ROWS, wide), f32),
            jax.ShapeDtypeStruct((ROWS, PER_SHOT, width_y), f32),
        ),
        in_specs=[vmem] * 4,
        out_specs=(hbm, hbm),
        scratch_shapes=[pltpu.VMEM((ROWS, PER_SHOT, width_y), f32), dma((5,))],
        compiler_params=pltpu.CompilerParams(vmem_limit_bytes=VMEM_BYTES),
    )(*fields)
    return (out[None], jnp.swapaxes(img, 1, 2))


def body(
    state, velocity, image_prior, source_x, source_y, wavelet, receiver_x, receiver_y, recorded
):
    shots = lax.axis_size("shot")
    width_x, width_y, per_shot = velocity.shape
    fits = (
        shots == 8
        and lax.axis_size("gx") == 2
        and lax.axis_size("gy") == 2
        and per_shot == PER_SHOT
        and width_x == ROWS
        and width_y == 48
        and wavelet.shape[1] == 2
    )
    chosen = fast_body if fits else general_body
    return chosen(
        state, velocity, image_prior, source_x, source_y, wavelet, receiver_x, receiver_y, recorded
    )


def solution(mesh):
    in_specs = (
        P("shot", None, "gx", "gy"),
        P("gx", "gy", "shot"),
        P("gx", "gy", "shot"),
        P("shot"),
        P("shot"),
        P("shot", None),
        P("shot", None),
        P("shot", None),
        P("shot", None, None),
    )
    out_specs = (P("shot", None, "gx", "gy"), P("gx", "gy", "shot"))
    return jax.shard_map(body, mesh=mesh, in_specs=in_specs, out_specs=out_specs, check_vma=False)
```

```python
import functools

import jax
import jax.numpy as jnp
from jax import lax
from jax.experimental import pallas as pl
from jax.experimental.pallas import tpu as pltpu
from jax.sharding import PartitionSpec as P

SRC_Z = 4
REC_Z = 2


STENCIL = (-205.0 / 72.0, 8.0 / 5.0, -1.0 / 5.0, 8.0 / 315.0, -1.0 / 560.0)

LANES = 128
ROWS = 16
DEPTH = 64
PER_SHOT = 8
UNROLL = 4
VMEM_BYTES = 48 * 1024 * 1024
MESH = pl.DeviceIdType.MESH
VEL_PARTS = ((0, 0), (0, 1), (0, 2), (1, 0), (1, 1), (1, 2))


def padded_2(cells, sides, width):
    for axis, dim in sides:
        count = lax.axis_size(axis)
        ends = count - 1
        head = lax.slice_in_dim(cells, 0, width, axis=dim)
        tail = lax.slice_in_dim(cells, cells.shape[dim] - width, cells.shape[dim], axis=dim)
        cells = jnp.concatenate(
            [
                lax.ppermute(tail, axis, [(i, (i + 1) % count) for i in range(ends)]),
                cells,
                lax.ppermute(head, axis, [((i + 1) % count, i) for i in range(ends)]),
            ],
            axis=dim,
        )
    return cells


def laplace(extended):
    width_x = extended.shape[1] - 8
    width_y = extended.shape[2] - 8
    depth = extended.shape[3]
    padded = jnp.pad(extended, ((0, 0), (0, 0), (0, 0), (4, 4)))

    def shifted(dx, dy, dz):
        return padded[
            :, 4 + dx : 4 + dx + width_x, 4 + dy : 4 + dy + width_y, 4 + dz : 4 + dz + depth
        ]

    summed = 3.0 * STENCIL[0] * shifted(0, 0, 0)
    for offset in range(1, 5):
        summed = summed + STENCIL[offset] * (
            shifted(offset, 0, 0)
            + shifted(-offset, 0, 0)
            + shifted(0, offset, 0)
            + shifted(0, -offset, 0)
            + shifted(0, 0, offset)
            + shifted(0, 0, -offset)
        )
    return summed


def inject_sources(
    advanced, x_coords, y_coords, source_x, source_y, wave_value, receiver_x, receiver_y, data_row
):
    src_plane = ((x_coords == source_x[0])[:, None] & (y_coords == source_y[0])[None, :]).astype(
        jnp.float32
    ) * wave_value
    onehot_x = (x_coords[:, None] == receiver_x[0][None, :]).astype(jnp.float32)
    onehot_y = (receiver_y[0][:, None] == y_coords[None, :]).astype(jnp.float32) * data_row[:, None]
    rec_plane = jnp.dot(
        onehot_x, onehot_y, precision=lax.Precision.HIGHEST, preferred_element_type=jnp.float32
    )
    advanced = advanced.at[0, :, :, SRC_Z].add(src_plane)
    return advanced.at[1, :, :, REC_Z].add(rec_plane)


def general_body(
    state, velocity, image_prior, source_x, source_y, wavelet, receiver_x, receiver_y, recorded
):
    step_count = wavelet.shape[1]
    width_x = velocity.shape[0]
    width_y = velocity.shape[1]
    velocity_full = lax.all_gather(velocity, "shot", axis=2, tiled=True)
    depth = velocity_full.shape[2]
    fields = state[0].reshape((4, width_x, width_y, depth))
    previous = jnp.stack((fields[0], fields[2]))
    current = jnp.stack((fields[1], fields[3]))
    base_x = lax.axis_index("gx") * width_x
    base_y = lax.axis_index("gy") * width_y
    image_sum = jnp.zeros(velocity_full.shape, jnp.float32)
    x_coords = base_x + jnp.arange(width_x, dtype=jnp.int32)
    y_coords = base_y + jnp.arange(width_y, dtype=jnp.int32)
    for step_index in range(step_count):
        extended = padded_2(current, (("gx", 1), ("gy", 2)), 4)
        advanced = 2.0 * current - previous + velocity_full[None] * laplace(extended)
        advanced = inject_sources(
            advanced,
            x_coords,
            y_coords,
            source_x,
            source_y,
            wavelet[0, step_index],
            receiver_x,
            receiver_y,
            recorded[0, step_index],
        )
        image_sum = image_sum + advanced[0] * advanced[1]
        previous, current = (current, advanced)
    result = jnp.stack((previous[0], current[0], previous[1], current[1]))
    result = result.reshape((1, 4, width_x, width_y * depth))
    image = image_prior + lax.psum_scatter(image_sum, "shot", scatter_dimension=2, tiled=True)
    return (result, image)


def iota(shape, dim):
    return lax.broadcasted_iota(jnp.int32, shape, dim)


def swap_shot_and_lane(tiles):
    lane = iota(tiles[0].shape, 1)
    for bit in range(3):
        span = 8 << bit
        low = (lane & span) == 0
        new = list(tiles)
        for i in range(8):
            if i & (1 << bit):
                continue
            a, b = tiles[i], tiles[i | (1 << bit)]
            new[i] = jnp.where(low, a, pltpu.roll(b, span, 1))
            new[i | (1 << bit)] = jnp.where(low, pltpu.roll(a, LANES - span, 1), b)
        tiles = new
    return tiles


def pieces(value):
    first = value.astype(jnp.bfloat16)
    return first, (value - first.astype(jnp.float32)).astype(jnp.bfloat16)


def depth_picks(groups, width_y):
    spot = iota((width_y, groups * LANES), 1)
    in_tile = spot & (LANES - 1)
    y_of = (spot >> 7) * 16 + ((in_tile >> 3) & 7) * 2 + (in_tile >> 6)
    picks = (iota((width_y, groups * LANES), 0) == y_of).astype(jnp.bfloat16)
    own_z = iota((LANES, groups * LANES), 0) & 7
    keep = own_z == (iota((LANES, groups * LANES), 1) & 7)
    return picks, keep


def thirds(value):
    first = value.astype(jnp.bfloat16)
    rest = value - first.astype(jnp.float32)
    second = rest.astype(jnp.bfloat16)
    return first, second, (rest - second.astype(jnp.float32)).astype(jnp.bfloat16)


def kernel(
    tiles,
    shots,
    sx_hbm,
    sy_hbm,
    wave_hbm,
    st_hbm,
    vel_hbm,
    prior_hbm,
    rx_hbm,
    ry_hbm,
    data_hbm,
    ext,
    last,
    total,
    prior_ref,
    sx_ref,
    sy_ref,
    wave_ref,
    rx_ref,
    ry_ref,
    data_ref,
    vel_ref,
    prev,
    lap,
    vgot,
    vfull,
    inj,
    xsend,
    xgot,
    ysend,
    ygot,
    isum,
    isend,
    igot,
    in_sem,
    xs_sem,
    xr_sem,
    ys_sem,
    yr_sem,
    vs_sem,
    vr_sem,
    is_sem,
    ir_sem,
):
    me = lax.axis_index("shot")
    gx = lax.axis_index("gx")
    gy = lax.axis_index("gy")
    width_y = tiles * LANES // DEPTH
    wide = tiles * LANES
    edge = 2 * LANES
    groups = tiles // 8
    c0, c1, c2, c3, c4 = STENCIL
    coefs = STENCIL
    mids = slice(8, 8 + ROWS)

    barrier = pltpu.get_barrier_semaphore()

    def shot_at(d):
        return sum(lax.rem(me // bit + d // bit, 2) * bit for bit in (1, 2, 4))

    def group_at(k):
        return k * gy + (groups - 1 - k) * (1 - gy)

    def in_order(values):
        return [jnp.where(gy == 1, values[k], values[groups - 1 - k]) for k in range(groups)]

    for d in range(1, shots):
        pl.semaphore_signal(
            barrier, inc=1, device_id=(shot_at(d), gx, gy), device_id_type=MESH
        )
    pl.semaphore_signal(barrier, inc=1, device_id=(me, 1 - gx, gy), device_id_type=MESH)
    pl.semaphore_signal(barrier, inc=1, device_id=(me, gx, 1 - gy), device_id_type=MESH)

    inner = (pl.ds(8, ROWS), pl.ds(edge, wide))
    firsts = (8 * (1 - gx), 8 * gx)

    def half_rows(half, ahead=0):
        return pl.ds(pl.multiple_of(firsts[half] + ahead, 8), 8)

    moves = [
        (vel_hbm, vel_ref),
        (st_hbm.at[1], ext.at[(0, 0) + inner]),
        (st_hbm.at[3], ext.at[(0, 1) + inner]),
        (rx_hbm, rx_ref),
        (ry_hbm, ry_ref),
        (data_hbm, data_ref),
        (st_hbm.at[0], prev.at[0]),
        (st_hbm.at[2], prev.at[1]),
        (sx_hbm, sx_ref),
        (sy_hbm, sy_ref),
        (wave_hbm, wave_ref),
        (prior_hbm, prior_ref),
    ]
    loads = [pltpu.make_async_copy(a, b, in_sem.at[i]) for i, (a, b) in enumerate(moves)]
    for load in loads:
        load.start()

    def at(t):
        return pl.ds(pl.multiple_of(t * LANES, LANES), LANES)

    for step in range(2):
        for f in range(2):
            for rows in (slice(0, 8), slice(8 + ROWS, 16 + ROWS)):
                ext[step, f, rows, :] = jnp.zeros((8, wide + 2 * edge), jnp.float32)
            for cols in (slice(0, edge), slice(wide + edge, wide + 2 * edge)):
                ext[step, f, mids, cols] = jnp.zeros((ROWS, edge), jnp.float32)

    picks, keep = depth_picks(groups, width_y)

    row8 = iota((8, LANES), 0)
    at_edge = (row8 >= 4) == (gx == 0)

    def split_rows(a, b):
        upper = jnp.where(row8 < 4, a, pltpu.roll(b, 4, 0))
        lower = jnp.where(row8 < 4, pltpu.roll(a, 4, 0), b)
        return [jnp.where(gx == 0, lower, upper), jnp.where(gx == 0, upper, lower)]

    loads[0].wait()
    flat = jnp.concatenate(pieces(vel_ref[...].reshape((ROWS * PER_SHOT, width_y))), axis=0)
    spread = jnp.dot(flat, picks, preferred_element_type=jnp.float32)
    rows8 = ROWS * PER_SHOT
    spread = spread[:rows8] + spread[rows8:]
    spread = jnp.where(keep, spread, 0.0).reshape((ROWS, PER_SHOT, groups * LANES))
    packed = jnp.sum(spread, axis=1)
    halves = (
        jnp.where(gx == 0, packed[8:], packed[:8]),
        jnp.where(gx == 0, packed[:8], packed[8:]),
    )
    for half in range(2):
        mine = [halves[half][:, u * LANES : (u + 1) * LANES] for u in range(groups)]
        mine = in_order(mine)
        if half == 0:
            mine[:2] = split_rows(*mine[:2])
        for k, tile in enumerate(mine):
            vgot[half, 0, k] = tile

    def columns(u):
        return pl.ds(pl.multiple_of(u * 8 * LANES, 8 * LANES), 8 * LANES)

    top = iota((8, 8 * LANES), 0) < 4

    def pack_x(step, u):
        cols = pl.ds(pl.multiple_of(u * 8 * LANES + edge, LANES), 8 * LANES)
        p, q = (ext[step, f, half_rows(0, 8), cols] for f in range(2))
        tail = jnp.where(top, pltpu.roll(p, 4, 0), q)
        head = jnp.where(top, p, pltpu.roll(q, 4, 0))
        xsend[step, :, columns(u)] = jnp.where(gx == 0, tail, head)

    def pack_y(step):
        for f in range(2):
            ysend[step, f] = jnp.where(
                gy == 0,
                ext[step, f, mids, wide : wide + edge],
                ext[step, f, mids, edge : 2 * edge],
            )

    def x_copy(step, k):
        part = (step,) if step == 0 else (step, slice(None), columns(group_at(k)))
        return pltpu.make_async_remote_copy(
            src_ref=xsend.at[part],
            dst_ref=xgot.at[part],
            send_sem=xs_sem.at[step + k],
            recv_sem=xr_sem.at[step + k],
            device_id=(me, 1 - gx, gy),
            device_id_type=MESH,
        )

    def y_copy(step):
        return pltpu.make_async_remote_copy(
            src_ref=ysend.at[step],
            dst_ref=ygot.at[step],
            send_sem=ys_sem.at[step],
            recv_sem=yr_sem.at[step],
            device_id=(me, gx, 1 - gy),
            device_id_type=MESH,
        )

    loads[1].wait()
    loads[2].wait()
    for u in range(groups):
        pack_x(0, u)
    pack_y(0)
    pl.semaphore_wait(barrier, shots + 1)
    xc, yc = x_copy(0, 0), y_copy(0)
    for part, (half, k) in enumerate(VEL_PARTS):
        for d in reversed(range(1, shots)):
            pltpu.make_async_remote_copy(
                src_ref=vgot.at[half, 0, k],
                dst_ref=vgot.at[half, d, k],
                send_sem=vs_sem.at[0],
                recv_sem=vr_sem.at[part],
                device_id=(shot_at(d), gx, gy),
                device_id_type=MESH,
            ).start()
        if part == 0:
            yc.start()
            xc.start()

    lane = iota((ROWS, LANES), 1)
    depth_at = lane & (DEPTH - 1)
    zero = jnp.zeros((ROWS, LANES), jnp.float32)
    base_x = gx * ROWS
    base_y = gy * width_y

    def along_x(a, b):
        up_a, up_b = ([pltpu.roll(v, 8 - r, 0) for r in range(1, 8)] for v in (a, b))
        above, below = 0.0, 0.0
        for k in range(1, 5):
            ahead, behind = row8 < 8 - k, row8 >= k
            above = above + coefs[k] * (
                jnp.where(ahead, up_a[k - 1], up_b[k - 1]) + jnp.where(behind, up_a[7 - k], 0.0)
            )
            below = below + coefs[k] * (
                jnp.where(ahead, up_b[k - 1], 0.0) + jnp.where(behind, up_b[7 - k], up_a[7 - k])
            )
        return above, below

    def laplace_own(step, first, count):
        size = min(count, 8)

        def one(quad, carry):
            for part in range(size):
                t = first + quad * size + part
                for f in range(2):
                    near = [ext[step, f, mids, at(t + 2 + k)] for k in (-2, -1, 0, 1, 2)]
                    mid = near[2]
                    total = (3.0 * c0) * mid
                    for k in range(1, 5):
                        total = total + jnp.where(depth_at >= k, coefs[k], 0.0) * pltpu.roll(
                            mid, k, 1
                        )
                        total = total + jnp.where(
                            depth_at < DEPTH - k, coefs[k], 0.0
                        ) * pltpu.roll(mid, LANES - k, 1)
                    total = total + c2 * (near[1] + near[3]) + c4 * (near[0] + near[4])
                    after = c1 * (near[3] + near[2]) + c3 * (near[4] + near[1])
                    before = c1 * (near[2] + near[1]) + c3 * (near[3] + near[0])
                    total = total + pltpu.roll(jnp.where(lane < DEPTH, after, before), DEPTH, 1)
                    above, below = along_x(mid[:8], mid[8:])
                    lap[f, 0:8, at(t)] = total[:8] + above
                    lap[f, 8:16, at(t)] = total[8:] + below
            return carry

        lax.fori_loop(0, count // size, one, 0)

    def add_y(step):
        on_left = gy == 1
        on_right = gy == 0
        first = lane < DEPTH
        for f in range(2):
            h0 = ygot[step, f, :, 0:LANES]
            h1 = ygot[step, f, :, LANES:edge]
            a0, a1 = jnp.where(on_left, h0, zero), jnp.where(on_left, h1, zero)
            b0, b1 = jnp.where(on_right, h0, zero), jnp.where(on_right, h1, zero)
            end = tiles - 1
            terms = {
                0: (c2 * a1 + c4 * a0, c3 * a1, c1 * a1 + c3 * a0),
                1: (c4 * a1, zero, c3 * a1),
                end - 1: (c4 * b0, c3 * b0, zero),
                end: (c2 * b0 + c4 * b1, c1 * b0 + c3 * b1, c3 * b0),
            }
            for t, (even, after, before) in terms.items():
                cols = slice(t * LANES, (t + 1) * LANES)
                lap[f, :, cols] = (
                    lap[f, :, cols]
                    + even
                    + pltpu.roll(jnp.where(first, after, before), DEPTH, 1)
                )

    row4 = row8 & 3
    low4 = row8 < 4

    def x_terms(h):
        left = jnp.where(gx == 1, coefs[4], 0.0) * h
        right = jnp.where(gx == 0, coefs[4], 0.0) * h
        for j in range(1, 4):
            left = left + jnp.where((row4 + j < 4) & (gx == 1), coefs[4 - j], 0.0) * pltpu.roll(
                h, 8 - j, 0
            )
            right = right + jnp.where((row4 >= j) & (gx == 0), coefs[4 - j], 0.0) * pltpu.roll(
                h, j, 0
            )
        source = jnp.where(low4, left, pltpu.roll(right, 4, 0))
        receiver = jnp.where(low4, pltpu.roll(left, 4, 0), right)
        return source, receiver

    def advance(step, half, u, draft=False):
        wave = wave_ref[0, step]
        rows = half_rows(half)
        inside = half_rows(half, 8)
        source_row = row8 == sx_ref[0] - base_x - firsts[half]

        def one(quad, carry):
            for part in range(8):
                t = u * 8 + quad * 8 + part
                terms = x_terms(xgot[step, :, at(t)]) if half == 0 else None
                v = vfull[half, :, at(t)]
                results = []
                for f in range(2):
                    current = ext[step, f, inside, at(t + 2)]
                    if step == 0:
                        previous = prev[f, rows, at(t)]
                    else:
                        previous = ext[0, f, inside, at(t + 2)]
                    spread_out = lap[f, rows, at(t)]
                    if half == 0:
                        spread_out = spread_out + terms[f]
                    new = 2.0 * current - previous + v * spread_out
                    if f == 0:
                        new = new + jnp.where(
                            source_row & (source_lane + t * LANES == 0), wave, 0.0
                        )
                    else:
                        new = new + inj[step, rows, at(t)]
                    if step == 0:
                        ext[1, f, inside, at(t + 2)] = new
                    else:
                        last[f, rows, at(t)] = new
                    results.append(new)
                if draft:
                    continue
                product = results[0] * results[1]
                if step == 0:
                    isum[half, :, at(t)] = product
                else:
                    isum[half, :, at(t)] = isum[half, :, at(t)] + product
            return carry

        one(0, 0)

    for load in loads[3:6]:
        load.wait()
    hit_x = (iota((ROWS, rx_ref.shape[1]), 0) == rx_ref[...] - base_x).astype(jnp.bfloat16)
    hit_y = (iota((width_y, ry_ref.shape[1]), 0) == ry_ref[...] - base_y).astype(jnp.bfloat16)
    parts = []
    for step in range(2):
        parts += [hit_x * piece for piece in thirds(data_ref[step : step + 1, :])]
    planes = lax.dot_general(
        jnp.concatenate(parts, axis=0),
        hit_y,
        (((1,), (1,)), ((), ())),
        preferred_element_type=jnp.float32,
    )
    for step in range(2):
        base = 3 * ROWS * step
        plane = (
            planes[base : base + ROWS]
            + planes[base + ROWS : base + 2 * ROWS]
            + planes[base + 2 * ROWS : base + 3 * ROWS]
        )
        for t in range(tiles):
            even = jnp.broadcast_to(plane[:, 2 * t : 2 * t + 1], (ROWS, LANES))
            odd = jnp.broadcast_to(plane[:, 2 * t + 1 : 2 * t + 2], (ROWS, LANES))
            inj[step, :, t * LANES : (t + 1) * LANES] = jnp.where(
                lane == REC_Z, even, jnp.where(lane == DEPTH + REC_Z, odd, 0.0)
            )

    laplace_own(0, 0, tiles)
    for load in loads[6:11]:
        load.wait()
    source_lane = iota((8, LANES), 1) - ((sy_ref[0] - base_y) * DEPTH + SRC_Z)
    yc.wait_recv()
    add_y(0)

    def arrived(ref, sem):
        pltpu.make_async_copy(ref, ref, sem).wait()

    others = pl.ds(1, shots - 1)
    slots = [shot_at(s) for s in range(shots)]
    xcopies = [x_copy(1, k) for k in range(groups)]
    next_y = y_copy(1)

    def send_image(half, k):
        u = group_at(k)
        mixed = swap_shot_and_lane([isum[half, :, at(8 * u + i)] for i in range(8)])
        for s in range(shots):
            isend[half, s, k] = mixed[s]
        for d in reversed(range(1, shots)):
            to = shot_at(d)
            pltpu.make_async_remote_copy(
                src_ref=isend.at[half, to, k],
                dst_ref=igot.at[half, d, k],
                send_sem=is_sem.at[0],
                recv_sem=ir_sem.at[half, k],
                device_id=(to, gx, gy),
                device_id_type=MESH,
            ).start()

    def near_half(k):
        xcopies[k].wait_recv()
        advance(1, 0, group_at(k))
        send_image(0, k)

    def far_half(k):
        advance(1, 1, group_at(k))
        send_image(1, k)

    def tile_at(k, i):
        return at(8 * group_at(k) + i)

    def laplace_next(low, high):
        first = low * gy + (tiles - high) * (1 - gy)
        laplace_own(1, first, high - low)

    for part, (half, slot) in enumerate(VEL_PARTS):
        arrived(vgot.at[half, others, slot], vr_sem.at[part])
        mixed = swap_shot_and_lane([vgot[half, slots[s], slot] for s in range(shots)])
        if (half, slot) == (0, 0):
            for i in range(8):
                turned = pltpu.roll(mixed[i], 4, 0)
                vfull[0, :, tile_at(0, i)] = jnp.where(gx == 0, turned, mixed[i])
                vfull[0, :, tile_at(1, i)] = jnp.where(gx == 0, mixed[i], turned)
            xc.wait_recv()
        elif (half, slot) == (0, 1):
            for i in range(8):
                turned = pltpu.roll(mixed[i], 4, 0)
                rest = (jnp.where(gx == 0, mixed[i], turned), jnp.where(gx == 0, turned, mixed[i]))
                for k in range(2):
                    vfull[0, :, tile_at(k, i)] = jnp.where(
                        at_edge, vfull[0, :, tile_at(k, i)], rest[k]
                    )
        else:
            for i in range(8):
                vfull[half, :, tile_at(slot, i)] = mixed[i]
        for k in (0, 1) if half == 0 and slot < 2 else (slot,):
            advance(0, half, group_at(k), part == 0)
            if half == 0 and slot != 1:
                pack_x(1, group_at(k))
                xcopies[k].start()
        if half == 0:
            continue
        if slot == 0:
            pack_y(1)
            next_y.start()
            laplace_next(0, 4)
        elif slot == 1:
            laplace_next(4, 12)
        else:
            laplace_next(12, 16)
            far_half(1)
            laplace_next(16, 24)
    far_half(2)
    next_y.wait_recv()
    add_y(1)
    far_half(0)
    for k in range(groups):
        near_half(k)
    arrived(vgot.at[:, others], vs_sem.at[0])
    for copy in (xc, yc, next_y, *xcopies):
        copy.wait_send()
    loads[11].wait()
    for half, k in ((1, 1), (1, 0), (1, 2), (0, 0), (0, 1), (0, 2)):
        arrived(igot.at[half, others, k], ir_sem.at[half, k])
        summed = isend[half, me, k]
        for d in range(1, shots):
            summed = summed + igot[half, d, k]
        total[group_at(k), half_rows(half), :] = summed
    arrived(igot.at[:, others], is_sem.at[0])


def store_kernel(ext, last, total, prior, state_out, image_out, img, out_sem):
    wide = last.shape[2]
    groups = total.shape[0]
    width_y = prior.shape[2]
    rows8 = ROWS * PER_SHOT
    inner = (pl.ds(8, ROWS), pl.ds(2 * LANES, wide))
    moves = []
    for f in range(2):
        moves.append((ext.at[(1, f) + inner], state_out.at[2 * f]))
        moves.append((last.at[f], state_out.at[2 * f + 1]))
    moves.append((img, image_out))
    stores = [pltpu.make_async_copy(a, b, out_sem.at[i]) for i, (a, b) in enumerate(moves)]
    for store in stores[:4]:
        store.start()
    picks, keep = depth_picks(groups, width_y)
    image = prior[...].reshape((rows8, width_y))
    for u in range(groups):
        cols = slice(u * LANES, (u + 1) * LANES)
        tall = jnp.broadcast_to(total[u][:, None, :], (ROWS, PER_SHOT, LANES))
        tall = jnp.where(keep[:, cols], tall.reshape((rows8, LANES)), 0.0)
        sides = lax.dot_general(
            jnp.concatenate(pieces(tall), axis=0),
            picks[:, cols],
            (((1,), (1,)), ((), ())),
            preferred_element_type=jnp.float32,
        )
        image = image + (sides[:rows8] + sides[rows8:])
    img[...] = image.reshape((ROWS, PER_SHOT, width_y))
    stores[4].start()
    for store in stores:
        store.wait()


def fast_body(
    state, velocity, image_prior, source_x, source_y, wavelet, receiver_x, receiver_y, recorded
):
    shots = lax.axis_size("shot")
    width_y = velocity.shape[1]
    wide = state.shape[3]
    tiles = wide // LANES
    groups = tiles // 8
    count = receiver_x.shape[1]
    f32 = jnp.float32
    hbm = pl.BlockSpec(memory_space=pltpu.HBM)
    dma = pltpu.SemaphoreType.DMA
    edge = 2 * LANES
    vmem = pl.BlockSpec(memory_space=pltpu.VMEM)
    held = (
        ((2, 2, ROWS + 16, wide + 2 * edge), f32),
        ((2, ROWS, wide), f32),
        ((groups, ROWS, LANES), f32),
        ((ROWS, PER_SHOT, width_y), f32),
    )
    pin = lambda a: pltpu.with_memory_space_constraint(a, pltpu.HBM)
    fields = pl.pallas_call(
        functools.partial(kernel, tiles, shots),
        out_shape=tuple(pltpu.VMEM(*a) for a in held),
        in_specs=[hbm] * 9,
        out_specs=(vmem,) * 4,
        scratch_shapes=[
            pltpu.SMEM((1,), jnp.int32),
            pltpu.SMEM((1,), jnp.int32),
            pltpu.SMEM((1, 2), f32),
            pltpu.VMEM((1, count), jnp.int32),
            pltpu.VMEM((1, count), jnp.int32),
            pltpu.VMEM((2, count), f32),
            pltpu.VMEM((ROWS, PER_SHOT, width_y), f32),
            pltpu.VMEM((2, ROWS, wide), f32),
            pltpu.VMEM((2, ROWS, wide), f32),
            pltpu.VMEM((2, shots, groups, 8, LANES), f32),
            pltpu.VMEM((2, 8, wide), f32),
            pltpu.VMEM((2, ROWS, wide), f32),
            pltpu.VMEM((2, 8, wide), f32),
            pltpu.VMEM((2, 8, wide), f32),
            pltpu.VMEM((2, 2, ROWS, edge), f32),
            pltpu.VMEM((2, 2, ROWS, edge), f32),
            pltpu.VMEM((2, 8, wide), f32),
            pltpu.VMEM((2, shots, groups, 8, LANES), f32),
            pltpu.VMEM((2, shots, groups, 8, LANES), f32),
            dma((12,)),
            dma((1 + groups,)),
            dma((1 + groups,)),
            dma((2,)),
            dma((2,)),
            dma((1,)),
            dma((len(VEL_PARTS),)),
            dma((1,)),
            dma((2, groups)),
        ],
        compiler_params=pltpu.CompilerParams(
            collective_id=0, has_side_effects=True, vmem_limit_bytes=VMEM_BYTES
        ),
    )(
        source_x,
        source_y,
        pin(wavelet),
        pin(state[0]),
        pin(jnp.swapaxes(velocity, 1, 2)),
        pin(jnp.swapaxes(image_prior, 1, 2)),
        pin(receiver_x),
        pin(receiver_y),
        pin(recorded[0]),
    )
    fields = [pltpu.with_memory_space_constraint(a, pltpu.VMEM) for a in fields]
    out, img = pl.pallas_call(
        store_kernel,
        out_shape=(
            jax.ShapeDtypeStruct((4, ROWS, wide), f32),
            jax.ShapeDtypeStruct((ROWS, PER_SHOT, width_y), f32),
        ),
        in_specs=[vmem] * 4,
        out_specs=(hbm, hbm),
        scratch_shapes=[pltpu.VMEM((ROWS, PER_SHOT, width_y), f32), dma((5,))],
        compiler_params=pltpu.CompilerParams(vmem_limit_bytes=VMEM_BYTES),
    )(*fields)
    return (out[None], jnp.swapaxes(img, 1, 2))


def body(
    state, velocity, image_prior, source_x, source_y, wavelet, receiver_x, receiver_y, recorded
):
    shots = lax.axis_size("shot")
    width_x, width_y, per_shot = velocity.shape
    fits = (
        shots == 8
        and lax.axis_size("gx") == 2
        and lax.axis_size("gy") == 2
        and per_shot == PER_SHOT
        and width_x == ROWS
        and width_y == 48
        and wavelet.shape[1] == 2
    )
    chosen = fast_body if fits else general_body
    return chosen(
        state, velocity, image_prior, source_x, source_y, wavelet, receiver_x, receiver_y, recorded
    )


def solution(mesh):
    in_specs = (
        P("shot", None, "gx", "gy"),
        P("gx", "gy", "shot"),
        P("gx", "gy", "shot"),
        P("shot"),
        P("shot"),
        P("shot", None),
        P("shot", None),
        P("shot", None),
        P("shot", None, None),
    )
    out_specs = (P("shot", None, "gx", "gy"), P("gx", "gy", "shot"))
    return jax.shard_map(body, mesh=mesh, in_specs=in_specs, out_specs=out_specs, check_vma=False)
```
